1024 devices in a mesh: elem: 128 (over x, z), span: 8 (over y, core).
Axes of the slice: x: 4, y: 4, z: 32, core: 2. Of those that a mesh axis runs over, the one named last changes fastest.
Arguments:
- adjoint: float32 [16384, 5, 512], P(('span', 'elem')), may hold values from -6 to 6
- density: float32 [16384], P(('span', 'elem')), may hold values from 0.5 to 2
- velocity: float32 [3, 16384], P(None, ('span', 'elem')), may hold values from -1.2 to 1.2
- pressure: float32 [16384], P(('span', 'elem')), may hold values from 0.4 to 1.6
- metric: float32 [3, 16384], P(None, ('span', 'elem')), may hold values from 0.5 to 2
- face_source: int32 [512, 4], P('elem'), may hold values from 0 to 23, as said below
- face_flip: int32 [512, 4], P('elem'), may hold values from 0 to 1, as said below
- face_tag: int32 [512, 4], P('elem'), may hold values from 0 to 2, as said below
- send_list: int32 [512, 2], P('elem'), may hold values from 0 to 15, as said below
Outputs:
- adjoint_next: float32 [16384, 5, 512], P(('span', 'elem'))
- register: float32 [16384, 5, 512], P(('span', 'elem'))
The draws below stay inside these ranges and needn't reach their ends.
Inputs may be any that keep to these rules, and one draw needn't show every extreme that they name: `face_source`: on an interior face the value names the neighbouring face as in the reference program; neighbours lie on the same partition or on partitions at most two away, periodic over 128; the named face names this one back; each entry of a partition's four received blocks is named by at most one face. On tagged faces the value is the face's own number 4 c + f. Some partition uses all 2 entries of its blocks to the partitions one and two after it in every draw. `face_flip`: equal on the two faces of an interior pair; 0 on tagged faces. `face_tag`: 0 interior, 1 slip wall, 2 far field; every partition has a tagged face. `send_list`: row 4 p + r lists faces of partition p, numbered 4 c + f; the first n of them, with 1 <= n <= 2, are the faces whose neighbours lie on partition p + (1, 2, -1, -2)[r], in the order in which that partition names them; the rest are named by no face.
All inputs are finite; a program needn't handle non-finite values.
Results may differ from the reference program's by a relative error of at most 0.000068.
Values sent between devices are 32-bit elements; how exact they have to be, the bound alone decides.
A program may use at most 32 MiB of HBM per device.

```python
import math
import jax
import jax.numpy as jnp
import numpy as np
from jax import lax

NV = 5
NODES = 512
COLS = 4
LAYERS = 4
SLOTS = 2
PARTS_SIZE = 128
ELEMS = 16384
N_SPAN = 8


def build_tables(key):
    subkeys = jax.random.split(jax.random.fold_in(key, 11), 7)
    face_count = 4 * COLS
    partitions = jnp.arange(PARTS_SIZE, dtype=jnp.int32)
    counts = jax.random.randint(subkeys[0], (PARTS_SIZE, 2), (SLOTS + 1) // 2, SLOTS + 1)
    chosen = jax.random.randint(subkeys[1], (), 0, PARTS_SIZE)
    counts = jnp.where((partitions == chosen)[:, None], SLOTS, counts)
    region_counts = jnp.stack([counts[:, 0], counts[:, 1], jnp.roll(counts[:, 0], 1), jnp.roll(counts[:, 1], 2)], axis=1)
    orders = jax.vmap(lambda subkey: jax.random.permutation(subkey, face_count))(jax.random.split(subkeys[2], PARTS_SIZE)).astype(jnp.int32)
    pair_bits = jax.random.randint(subkeys[3], (PARTS_SIZE, 2, SLOTS), 0, 2)
    region_bits = jnp.stack([pair_bits[:, 0], pair_bits[:, 1], jnp.roll(pair_bits[:, 0], 1, axis=0), jnp.roll(pair_bits[:, 1], 2, axis=0)], axis=1)
    position = jnp.arange(face_count, dtype=jnp.int32)
    region = jnp.minimum(position // SLOTS, 3)
    within = position % SLOTS
    in_front = position < 4 * SLOTS
    is_remote = in_front[None, :] & (within[None, :] < region_counts[:, region])
    opposite = jnp.array([2, 3, 0, 1], dtype=jnp.int32)
    remote_source = 4 * COLS + opposite[region] * SLOTS + within
    remote_flip = region_bits[:, region, within]
    rest_flag = 1 - is_remote.astype(jnp.int32)
    ranking = jnp.cumsum(rest_flag, axis=1) - 1
    rest_total = jnp.sum(rest_flag, axis=1)
    border = jax.random.randint(subkeys[4], (PARTS_SIZE,), 1, COLS // 2 + 1)
    border = border + (rest_total - border) % 2
    rest_order = jnp.argsort(is_remote.astype(jnp.int32), axis=1, stable=True).astype(jnp.int32)
    mate_rank = jnp.bitwise_xor(ranking - border[:, None], 1) + border[:, None]
    mate_rank = jnp.clip(mate_rank, 0, face_count - 1)
    mate_position = jnp.take_along_axis(rest_order, mate_rank, axis=1)
    mate_slot = jnp.take_along_axis(orders, mate_position, axis=1)
    on_border = (rest_flag == 1) & (ranking < border[:, None])
    local_bits = jax.random.randint(subkeys[5], (PARTS_SIZE, face_count), 0, 2)
    local_flip = jnp.take_along_axis(local_bits, jnp.clip((ranking - border[:, None]) // 2, 0, face_count - 1), axis=1)
    border_tag = jax.random.randint(subkeys[6], (PARTS_SIZE, face_count), 1, 3)
    source_at = jnp.where(is_remote, remote_source[None, :], jnp.where(on_border, orders, mate_slot))
    flip_at = jnp.where(is_remote, remote_flip, jnp.where(on_border, 0, local_flip))
    tag_at = jnp.where(on_border, border_tag, 0)
    inverse = jnp.argsort(orders, axis=1).astype(jnp.int32)
    source_table = jnp.take_along_axis(source_at, inverse, axis=1).reshape(PARTS_SIZE * COLS, 4)
    flip_table = jnp.take_along_axis(flip_at, inverse, axis=1).reshape(PARTS_SIZE * COLS, 4)
    tag_table = jnp.take_along_axis(tag_at, inverse, axis=1).reshape(PARTS_SIZE * COLS, 4)
    send_table = orders[:, :4 * SLOTS].reshape(PARTS_SIZE * 4, SLOTS)
    return (source_table.astype(jnp.int32), flip_table.astype(jnp.int32), tag_table.astype(jnp.int32), send_table.astype(jnp.int32))


def draw_face_source(key, part):
    return build_tables(key)[0]


def draw_face_flip(key, part):
    return build_tables(key)[1]


def draw_face_tag(key, part):
    return build_tables(key)[2]


def draw_send_list(key, part):
    return build_tables(key)[3]


def block_levels(stream_key, extent, shards, least, top_value):
    factor_of = 1.0
    for dim, parts in shards:
        heights = jax.random.uniform(jax.random.fold_in(jax.random.fold_in(stream_key, 6), dim), (parts,), jnp.float32, least / len(shards), top_value / len(shards))
        factor_of = factor_of * jnp.repeat(jnp.exp(heights), extent[dim] // parts).reshape((-1,) + (1,) * (len(extent) - 1 - dim))
    return factor_of


def noise(key, dims, scale, bound, shards=(), held_as=jnp.bfloat16):
    entries = jax.random.normal(key, dims, jnp.float32) * scale
    if len(shards) > 0:
        entries = block_levels(key, dims, shards, -0.22, 0.18) * entries
    return jnp.clip(entries, min=-bound, max=bound).astype(held_as)


def setup_inputs(seed: int = 0) -> dict:
    arg_keys = jax.random.split(jax.random.key(seed), 10)
    adjoint = noise(arg_keys[0], (ELEMS, NV, NODES), 1.0, 6.0, ((0, 1024),), jnp.float32)
    density = jnp.clip(jnp.exp(math.log(2.0) - 1.3862944 * jax.random.uniform(arg_keys[1], (ELEMS,), jnp.float32) ** block_levels(arg_keys[1], (ELEMS,), ((0, 1024),), -0.2, 0.2)), 0.5, 2.0)
    velocity = noise(arg_keys[2], (3, ELEMS), 0.4, 1.2, ((1, 1024),), jnp.float32)
    pressure = jnp.clip(jnp.exp(math.log(1.6) - 1.3862944 * jax.random.uniform(arg_keys[3], (ELEMS,), jnp.float32) ** block_levels(arg_keys[3], (ELEMS,), ((0, 1024),), -0.2, 0.2)), 0.4, 1.6)
    metric = jnp.clip(jnp.exp(math.log(2.0) - 1.3862944 * jax.random.uniform(arg_keys[4], (3, ELEMS), jnp.float32) ** block_levels(arg_keys[4], (3, ELEMS), ((1, 1024),), -0.2, 0.2)), 0.5, 2.0)
    face_source = draw_face_source(jax.random.fold_in(arg_keys[9], 71), 0)
    face_flip = draw_face_flip(jax.random.fold_in(arg_keys[9], 71), 0)
    face_tag = draw_face_tag(jax.random.fold_in(arg_keys[9], 71), 0)
    send_list = draw_send_list(jax.random.fold_in(arg_keys[9], 71), 0)
    return {"adjoint": adjoint, "density": density, "velocity": velocity, "pressure": pressure, "metric": metric, "face_source": face_source, "face_flip": face_flip, "face_tag": face_tag, "send_list": send_list}


gamma_gas = 1.4
lift_end = 28.0
time_step = 0.02
section_a2 = -567301805773.0 / 1357537059087.0
section_b1 = 1432997174477.0 / 9575080441755.0
section_b2 = 5161836677717.0 / 13612068292357.0

def lobatto_nodes():
    return [-1.0, -0.8717401485096066, -0.5917001814331423, -0.2092992179024789, 0.2092992179024789, 0.5917001814331423, 0.8717401485096066, 1.0]

def lobatto_derivative():
    positions = np.array(lobatto_nodes())
    total_nodes = positions.shape[0]
    differences = positions[:, None] - positions[None, :] + np.eye(total_nodes)
    weights = 1.0 / np.prod(differences, axis=1)
    matrix_out = weights[None, :] / weights[:, None] / differences
    matrix_out = matrix_out * (1.0 - np.eye(total_nodes))
    return matrix_out - np.eye(total_nodes) * np.sum(matrix_out, axis=1)[:, None]

def wall_table(columns):
    signs = np.ones((4, 5, 64))
    for face_index in range(4):
        signs[face_index, 1 + face_index // 2, :] = -1.0
    return np.tile(signs.reshape(4, 320), (columns, 1))

def adjoint_flux(values, direction, density_c, along, stiffness):
    components = [along * values[..., component, :] for component in range(5)]
    components[1 + direction] = components[1 + direction] + density_c * values[..., 0, :] + stiffness * values[..., 4, :]
    components[4] = components[4] + values[..., 1 + direction, :] / density_c
    return jnp.stack(components, axis=-2)

def volume_terms(derivatives, density_c, velocity_c, pressure_c, metric_c):
    stiffness = gamma_gas * pressure_c
    terms_list = [metric_c[direction][..., None] * adjoint_flux(derivatives[direction], direction, density_c, velocity_c[direction], stiffness) for direction in range(3)]
    return terms_list[0] + terms_list[1] + terms_list[2]

def face_terms(difference, density_c, velocity_c, pressure_c, metric_c):
    stiffness = gamma_gas * pressure_c
    sound = jnp.sqrt(stiffness / density_c)
    signs = jnp.concatenate([-jnp.ones((64,), jnp.float32), jnp.ones((64,), jnp.float32)])
    pieces = []
    for direction in range(3):
        block_in = difference[:, :, 128 * direction:128 * direction + 128]
        flux_out = adjoint_flux(block_in, direction, density_c, velocity_c[direction], stiffness)
        speed = jnp.abs(velocity_c[direction]) + sound
        pieces.append(0.5 * lift_end * metric_c[direction][..., None] * (signs * flux_out + speed[..., None] * block_in))
    return jnp.concatenate(pieces, axis=2)

def reference(adjoint, density, velocity, pressure, metric, face_source, face_flip, face_tag, send_list):
    span_layers = N_SPAN * LAYERS
    slab_columns = COLS * PARTS_SIZE
    face_total = 4 * COLS
    highest = lax.Precision.HIGHEST

    def to_layers(values):
        trailing = values.shape[1:]
        shaped = values.reshape((N_SPAN, PARTS_SIZE, LAYERS, COLS) + trailing)
        shaped = jnp.swapaxes(shaped, 1, 2)
        return shaped.reshape((span_layers, slab_columns) + trailing)

    def from_layers(values):
        trailing = values.shape[2:]
        shaped = values.reshape((N_SPAN, LAYERS, PARTS_SIZE, COLS) + trailing)
        shaped = jnp.swapaxes(shaped, 1, 2)
        return shaped.reshape((ELEMS,) + trailing)
    density_layers = to_layers(density)
    velocity_layers = to_layers(jnp.transpose(velocity))
    pressure_layers = to_layers(pressure)
    metric_layers = to_layers(jnp.transpose(metric))
    sources = face_source.reshape(PARTS_SIZE, face_total)
    partition = jnp.arange(PARTS_SIZE, dtype=jnp.int32)[:, None]
    remote = sources >= face_total
    region = jnp.where(remote, (sources - face_total) // SLOTS, 0).astype(jnp.int32)
    within = jnp.where(remote, (sources - face_total) % SLOTS, 0).astype(jnp.int32)
    offsets = jnp.array([1, 2, -1, -2], dtype=jnp.int32)
    sender = ((partition - offsets[region]) % PARTS_SIZE).astype(jnp.int32)
    send_rows = send_list.reshape(PARTS_SIZE, 4, SLOTS)
    partner_face = send_rows[sender, region, within]
    partner = jnp.where(remote, sender * face_total + partner_face, partition * face_total + sources).reshape(-1).astype(jnp.int32)
    flip_mask = (face_flip.reshape(-1) == 1)[None, :, None]
    tag_mask = face_tag.reshape(-1)[None, :, None]
    wall_sign = jnp.asarray(wall_table(slab_columns), jnp.float32)
    derivative = jnp.asarray(lobatto_derivative(), jnp.float32)

    def one_layer(inputs):
        layer_state, layer_difference, density_c, velocity_c, pressure_c, metric_c = inputs
        nodal_cube = layer_state.reshape(slab_columns, 5, 8, 8, 8)
        along_x = jnp.einsum('ip,nvkjp->nvkji', derivative, nodal_cube, precision=highest)
        along_y = jnp.einsum('jp,nvkpi->nvkji', derivative, nodal_cube, precision=highest)
        along_z = jnp.einsum('kp,nvpji->nvkji', derivative, nodal_cube, precision=highest)
        derivatives = [along_x.reshape(slab_columns, 5, 512), along_y.reshape(slab_columns, 5, 512), along_z.reshape(slab_columns, 5, 512)]
        density_col = density_c[:, None]
        velocity_col = [velocity_c[:, direction][:, None] for direction in range(3)]
        pressure_col = pressure_c[:, None]
        metric_col = [metric_c[:, direction][:, None] for direction in range(3)]
        volume = volume_terms(derivatives, density_col, velocity_col, pressure_col, metric_col)
        surface = face_terms(layer_difference, density_col, velocity_col, pressure_col, metric_col)
        pieces = [surface[:, :, 64 * face_index:64 * face_index + 64].reshape(slab_columns, 5, 8, 8) for face_index in range(6)]
        assembled = volume.reshape(slab_columns, 5, 8, 8, 8)
        assembled = assembled.at[:, :, :, :, 0].add(pieces[0])
        assembled = assembled.at[:, :, :, :, 7].add(pieces[1])
        assembled = assembled.at[:, :, :, 0, :].add(pieces[2])
        assembled = assembled.at[:, :, :, 7, :].add(pieces[3])
        assembled = assembled.at[:, :, 0].add(pieces[4])
        assembled = assembled.at[:, :, 7].add(pieces[5])
        return assembled.reshape(slab_columns, 5, 512)

    def residual(current):
        nodal_cube = current.reshape(span_layers, slab_columns, 5, 8, 8, 8)
        faces_list = [nodal_cube[..., 0], nodal_cube[..., 7], nodal_cube[..., 0, :], nodal_cube[..., 7, :], nodal_cube[:, :, :, 0], nodal_cube[:, :, :, 7]]
        traces = jnp.concatenate([face_block.reshape(span_layers, slab_columns, 5, 64) for face_block in faces_list], axis=3)
        in_plane = traces[..., :256].reshape(span_layers, slab_columns, 5, 4, 64)
        in_plane = jnp.swapaxes(in_plane, 2, 3).reshape(span_layers, 4 * slab_columns, 320)
        exterior = jnp.take(in_plane, partner, axis=1)
        mirrored = exterior.reshape(span_layers, 4 * slab_columns, 5, 8, 8)[..., ::-1].reshape(span_layers, 4 * slab_columns, 320)
        exterior = jnp.where(flip_mask, mirrored, exterior)
        exterior = jnp.where(tag_mask == 0, exterior, jnp.where(tag_mask == 1, in_plane * wall_sign, jnp.zeros_like(exterior)))
        outer_plane = jnp.swapaxes(exterior.reshape(span_layers, slab_columns, 4, 5, 64), 2, 3).reshape(span_layers, slab_columns, 5, 256)
        from_below = jnp.roll(traces[..., 320:], 1, axis=0)
        from_above = jnp.roll(traces[..., 256:320], -1, axis=0)
        difference = jnp.concatenate([outer_plane, from_below, from_above], axis=3) - traces
        return lax.map(one_layer, (current, difference, density_layers, velocity_layers, pressure_layers, metric_layers))
    start_state = to_layers(adjoint)
    section_one = time_step * residual(start_state)
    middle = start_state + section_b1 * section_one
    register = section_a2 * section_one + time_step * residual(middle)
    section_end = middle + section_b2 * register
    return (from_layers(section_end), from_layers(register))
```

```python
import functools

import jax
import jax.numpy as jnp
import numpy as np
from jax import lax
from jax.experimental import pallas as pl
from jax.experimental.pallas import tpu as pltpu
from jax.sharding import PartitionSpec as P

gamma_gas = 1.4
lift_end = 28.0
time_step = 0.02
section_a2 = -567301805773.0 / 1357537059087.0
section_b1 = 1432997174477.0 / 9575080441755.0
section_b2 = 5161836677717.0 / 13612068292357.0
offsets = (1, 2, -1, -2)
MESH = pl.DeviceIdType.MESH


def lobatto_derivative():
    positions = np.array(
        [
            -1.0,
            -0.8717401485096066,
            -0.5917001814331423,
            -0.2092992179024789,
            0.2092992179024789,
            0.5917001814331423,
            0.8717401485096066,
            1.0,
        ]
    )
    total_nodes = positions.shape[0]
    differences = positions[:, None] - positions[None, :] + np.eye(total_nodes)
    weights = 1.0 / np.prod(differences, axis=1)
    matrix_out = weights[None, :] / weights[:, None] / differences
    matrix_out = matrix_out * (1.0 - np.eye(total_nodes))
    return matrix_out - np.eye(total_nodes) * np.sum(matrix_out, axis=1)[:, None]


def plane_table():
    matrix_in = lobatto_derivative()
    along_x = np.kron(np.eye(16), matrix_in).T
    along_y = np.kron(np.eye(2), np.kron(matrix_in, np.eye(8))).T
    table = np.concatenate([along_x, along_y], axis=1).astype(np.float32)
    high = table.astype(jnp.bfloat16)
    low = (table - high.astype(np.float32)).astype(jnp.bfloat16)
    return np.concatenate([high, high, low], axis=0)


def depth_table():
    matrix_in = lobatto_derivative()
    table = np.zeros((4, 4, 2, 128))
    for out_tile in range(4):
        for in_tile in range(4):
            table[out_tile, in_tile, 0, :64] = matrix_in[2 * out_tile, 2 * in_tile]
            table[out_tile, in_tile, 0, 64:] = matrix_in[2 * out_tile + 1, 2 * in_tile + 1]
            table[out_tile, in_tile, 1, :64] = matrix_in[2 * out_tile, 2 * in_tile + 1]
            table[out_tile, in_tile, 1, 64:] = matrix_in[2 * out_tile + 1, 2 * in_tile]
    return table.reshape(32, 128).astype(np.float32)


def along_axis(values, index, axis):
    rest = tuple(a for a in range(values.ndim) if a != axis)
    numbers = lax.GatherDimensionNumbers(
        offset_dims=(),
        collapsed_slice_dims=(axis,),
        start_index_map=(axis,),
        operand_batching_dims=rest,
        start_indices_batching_dims=rest,
    )
    index = jnp.broadcast_to(index, values.shape)
    return lax.gather(
        values,
        index[..., None],
        numbers,
        slice_sizes=(1,) * values.ndim,
        mode=lax.GatherScatterMode.PROMISE_IN_BOUNDS,
    )


def lanes(values, index):
    return along_axis(values, index, values.ndim - 1)


def rows(values, index):
    return along_axis(values, index, values.ndim - 2)


def kernel(
    adj_hbm, rho_hbm, vel_hbm, pres_hbm, met_hbm, src_hbm, flip_hbm, tag_hbm, send_hbm, plane_hbm, depth_hbm,
    next_hbm, reg_hbm,
    q_ref, mid_ref, keep_ref, acc_ref, out_ref,
    rho_ref, vel_ref, pres_ref, met_ref, src_ref, flip_ref, tag_ref, send_ref, plane_ref, depth_ref,
    tx_ref, tz_ref, rx_ref, rz_ref,
    in_sem, out_sem, tx_sem, rx_sem,
):
    n_elem, n_span = lax.axis_size("elem"), lax.axis_size("span")
    part, slab = lax.axis_index("elem"), lax.axis_index("span")
    peers = [{"elem": lax.rem(part + n_elem + o, n_elem)} for o in offsets]
    peers += [{"span": lax.rem(slab + n_span + o, n_span)} for o in (1, -1)]

    barrier = pltpu.get_barrier_semaphore()
    for peer in peers:
        pl.semaphore_signal(barrier, inc=1, device_id=peer, device_id_type=MESH)

    loads = [
        pltpu.make_async_copy(src, dst, in_sem.at[i])
        for i, (src, dst) in enumerate(
            [
                (send_hbm, send_ref), (adj_hbm, q_ref), (plane_hbm, plane_ref), (depth_hbm, depth_ref),
                (rho_hbm, rho_ref), (vel_hbm, vel_ref), (pres_hbm, pres_ref), (met_hbm, met_ref),
                (src_hbm, src_ref), (flip_hbm, flip_ref), (tag_hbm, tag_ref),
            ]
        )
    ]
    for load in loads:
        load.start()

    lane = lax.broadcasted_iota(jnp.int32, (8, 128), 1)
    row = lax.broadcasted_iota(jnp.int32, (8, 128), 0)
    half, place = lane >> 6, lane & 63
    first_half = half == 0
    low_rows = row < 4
    column, group = row & 3, row & 4
    from_x = ((lane >> 3) & 1) * 64 + (lane & 7) * 8 + 7 * half
    from_y = ((lane >> 3) & 1) * 64 + 56 * half + (lane & 7)
    quarter = place >> 4
    node_i, node_j, node_k = lane & 7, (lane >> 3) & 7, lane >> 6
    to_x = 64 * (node_i >> 2) + 8 * node_k + node_j
    to_y = 64 * (node_j >> 2) + 8 * node_k + node_i
    on_x = (node_i == 0) | (node_i == 7)
    on_y = (node_j == 0) | (node_j == 7)

    def tiles_of(ref):
        return [ref[:, :, 128 * t : 128 * t + 128].reshape(10, 8, 128) for t in range(4)]

    def traces(q):
        pair_x, pair_y = lanes(q[0], from_x), lanes(q[0], from_y)
        for t in range(1, 4):
            pair_x = jnp.where(quarter == t, lanes(q[t], from_x), pair_x)
            pair_y = jnp.where(quarter == t, lanes(q[t], from_y), pair_y)
        return pair_x, pair_y, jnp.where(first_half, q[0], q[3])

    def picked(pair_x, pair_y, face):
        index = group + ((face >> 2) & 3)
        return jnp.where((face & 2) == 0, rows(pair_x, index), rows(pair_y, index))

    def send(pair_x, pair_y, swapped, turned, send_faces, turn):
        outs = [
            lanes(picked(pair_x, pair_y, face), 64 * (face & 1) + place) for face in send_faces
        ]
        out = jnp.where(first_half, outs[0], outs[1])
        for j in range(3):
            q = [out[min(4 * j + i, 9)] for i in range(4)]
            odd = (row & 1) == 1
            q = [
                jnp.where(odd, pltpu.roll(q[1], 1, 0), q[0]),
                jnp.where(odd, q[1], pltpu.roll(q[0], 7, 0)),
                jnp.where(odd, pltpu.roll(q[3], 1, 0), q[2]),
                jnp.where(odd, q[3], pltpu.roll(q[2], 7, 0)),
            ]
            upper = (row & 2) == 2
            q = [
                jnp.where(upper, pltpu.roll(q[2], 2, 0), q[0]),
                jnp.where(upper, pltpu.roll(q[3], 2, 0), q[1]),
                jnp.where(upper, q[2], pltpu.roll(q[0], 6, 0)),
                jnp.where(upper, q[3], pltpu.roll(q[1], 6, 0)),
            ]
            for r in range(4):
                tx_ref[turn, r, j] = q[r]
            v0, v1 = 2 * j, min(2 * j + 1, 4)
            tz_ref[turn, 0, j] = jnp.where(low_rows, turned[2 * v0 + 1], swapped[2 * v1 + 1])
            tz_ref[turn, 1, j] = jnp.where(low_rows, swapped[2 * v0], turned[2 * v1])

    def copies(turn):
        return [
            pltpu.make_async_remote_copy(
                src_ref=tx_ref.at[turn, i] if i < 4 else tz_ref.at[turn, i - 4],
                dst_ref=rx_ref.at[turn, i] if i < 4 else rz_ref.at[turn, i - 4],
                send_sem=tx_sem.at[turn, i],
                recv_sem=rx_sem.at[turn, i],
                device_id=peers[i],
                device_id_type=MESH,
            )
            for i in range(6)
        ]

    def volume(q, acc):
        sides = []
        for t in range(4):
            flat = q[t].reshape(80, 128)
            high = flat.astype(jnp.bfloat16)
            low = (flat - high.astype(jnp.float32)).astype(jnp.bfloat16)
            sides.append(jnp.concatenate([high, low, high], axis=1))
        plane = jnp.dot(
            jnp.concatenate(sides, axis=0), plane_ref[...], preferred_element_type=jnp.float32
        )
        rolled = [pltpu.roll(tile, 64, 2) for tile in q]
        for t in range(4):
            depth = None
            for s in range(4):
                for part_in, tile in ((0, q[s]), (1, rolled[s])):
                    at = (t * 4 + s) * 2 + part_in
                    term = depth_ref[at : at + 1, :] * tile
                    depth = term if depth is None else depth + term
            flat = plane[80 * t : 80 * t + 80]
            slopes = [
                flat[:, :128].reshape(5, 2, 8, 128),
                flat[:, 128:].reshape(5, 2, 8, 128),
                depth.reshape(5, 2, 8, 128),
            ]
            total = [
                along[0] * slopes[0][v] + along[1] * slopes[1][v] + along[2] * slopes[2][v]
                for v in range(5)
            ]
            for d in range(3):
                total[1 + d] = total[1 + d] + by_rho[d] * slopes[d][0] + by_stiff[d] * slopes[d][4]
                total[4] = total[4] + by_inverse[d] * slopes[d][1 + d]
            for v in range(5):
                acc[v, :, 128 * t : 128 * t + 128] = total[v].reshape(16, 128)

    def surface(d, difference):
        g = difference.reshape(5, 2, 8, 128)
        out = [face_all[d] * g[v] for v in range(5)]
        out[1 + d] = out[1 + d] + face_rho[d] * g[0] + face_stiff[d] * g[4]
        out[4] = out[4] + face_inverse[d] * g[1 + d]
        return jnp.stack(out, axis=0).reshape(10, 8, 128)

    def lifted(locals_in, pair_x, pair_y, pair_z, turned, turn):
        remote = []
        for r in range(4):
            boxes = [rx_ref[turn, r, j] for j in range(3)]
            remote.append(
                jnp.stack([rows(boxes[vh >> 2], group + (vh & 3)) for vh in range(10)], axis=0)
            )
        pieces = []
        for d, own in ((0, pair_x), (1, pair_y)):
            sides = []
            for f in (2 * d, 2 * d + 1):
                face = sources[f]
                chosen = locals_in[f]
                for r in range(4):
                    chosen = jnp.where((face >> 1) == 8 + r, remote[r], chosen)
                sides.append(lanes(chosen, 64 * (face & 1) + (place ^ (7 * flips[f]))))
            outer = jnp.where(first_half, sides[0], sides[1])
            tag = jnp.where(first_half, tags[2 * d], tags[2 * d + 1])
            plain = jnp.where(tag == 1, 0.0, -1.0)
            normal = jnp.where(tag == 1, -2.0, -1.0)
            own5, outer5 = own.reshape(5, 2, 8, 128), outer.reshape(5, 2, 8, 128)
            difference = jnp.stack(
                [
                    jnp.where(
                        tag == 0, outer5[v] - own5[v], (normal if v == 1 + d else plain) * own5[v]
                    )
                    for v in range(5)
                ],
                axis=0,
            )
            pieces.append(surface(d, difference))
        outers = []
        for v in range(5):
            below, above = rz_ref[turn, 0, v >> 1], rz_ref[turn, 1, v >> 1]
            if v & 1:
                below = pltpu.roll(below, 4, 0)
            else:
                above = pltpu.roll(above, 4, 0)
            t0, t1 = turned[2 * v], turned[2 * v + 1]
            inner = jnp.where(low_rows, t0, t1)
            outers.append(jnp.where(first_half, jnp.where(low_rows, below, t0), inner))
            outers.append(jnp.where(first_half, inner, jnp.where(low_rows, t1, above)))
        piece_z = surface(2, jnp.stack(outers, axis=0) - pair_z)
        result = []
        for t in range(4):
            total = jnp.where(on_x, lanes(pieces[0], to_x + 16 * t), 0.0) + jnp.where(
                on_y, lanes(pieces[1], to_y + 16 * t), 0.0
            )
            if t == 0:
                total = total + jnp.where(first_half, piece_z, 0.0)
            if t == 3:
                total = total + jnp.where(first_half, 0.0, piece_z)
            result.append(total)
        return result

    loads[0].wait()
    loads[1].wait()
    send_faces = []
    for k in range(2):
        face = jnp.zeros((8, 128), jnp.int32)
        for r in range(4):
            face = jnp.where(column == r, send_ref[k : k + 1, r : r + 1], face)
        send_faces.append(face)
    q = tiles_of(q_ref)
    pair_x, pair_y, pair_z = traces(q)
    swapped = pltpu.roll(pair_z, 64, 2)
    turned = pltpu.roll(swapped, 4, 1)
    send(pair_x, pair_y, swapped, turned, send_faces, 0)
    pl.semaphore_wait(barrier, 6)
    first = copies(0)
    for copy in first:
        copy.start()

    for load in loads[2:]:
        load.wait()
    sixteen = lax.broadcasted_iota(jnp.int32, (16, 16), 0) == lax.broadcasted_iota(jnp.int32, (16, 16), 1)

    def upright(line):
        spread = jnp.where(sixteen, jnp.broadcast_to(line, (16, 16)), 0.0)
        return jnp.broadcast_to(jnp.sum(spread, axis=1, keepdims=True), (16, 128)).reshape(2, 8, 128)

    rho, pressure = upright(rho_ref[...]), upright(pres_ref[...])
    stiff = gamma_gas * pressure
    inverse = 1.0 / rho
    sound = jnp.sqrt(stiff / rho)
    sign = jnp.where(first_half, -0.5 * lift_end, 0.5 * lift_end)
    along, by_rho, by_stiff, by_inverse = [], [], [], []
    face_all, face_rho, face_stiff, face_inverse = [], [], [], []
    for d in range(3):
        speed = upright(vel_ref[d : d + 1, :])
        scale = time_step * upright(met_ref[d : d + 1, :])
        along.append(scale * speed)
        by_rho.append(scale * rho)
        by_stiff.append(scale * stiff)
        by_inverse.append(scale * inverse)
        face_all.append(sign * along[d] + 0.5 * lift_end * scale * (jnp.abs(speed) + sound))
        face_rho.append(sign * by_rho[d])
        face_stiff.append(sign * by_stiff[d])
        face_inverse.append(sign * by_inverse[d])

    def spread_column(ref, f):
        one = jnp.broadcast_to(ref[:, f : f + 1], (4, 128))
        return jnp.concatenate([one, one], axis=0)

    sources = [spread_column(src_ref, f) for f in range(4)]
    flips = [spread_column(flip_ref, f) for f in range(4)]
    tags = [spread_column(tag_ref, f) for f in range(4)]

    locals_in = [picked(pair_x, pair_y, sources[f]) for f in range(4)]
    volume(q, acc_ref)
    for copy in first:
        copy.wait_recv()
    surf = lifted(locals_in, pair_x, pair_y, pair_z, turned, 0)
    middle = []
    for t in range(4):
        at = slice(128 * t, 128 * t + 128)
        section = acc_ref[:, :, at].reshape(10, 8, 128) + surf[t]
        middle.append(q_ref[:, :, at].reshape(10, 8, 128) + section_b1 * section)
        mid_ref[:, :, at] = middle[t].reshape(5, 16, 128)
        keep_ref[:, :, at] = (section_a2 * section).reshape(5, 16, 128)

    pair_x, pair_y, pair_z = traces(middle)
    swapped = pltpu.roll(pair_z, 64, 2)
    turned = pltpu.roll(swapped, 4, 1)
    send(pair_x, pair_y, swapped, turned, send_faces, 1)
    second = copies(1)
    for copy in second:
        copy.start()
    locals_in = [picked(pair_x, pair_y, sources[f]) for f in range(4)]
    volume(middle, acc_ref)
    for copy in second:
        copy.wait_recv()
    surf = lifted(locals_in, pair_x, pair_y, pair_z, turned, 1)
    for t in range(4):
        at = slice(128 * t, 128 * t + 128)
        register = (keep_ref[:, :, at] + acc_ref[:, :, at]).reshape(10, 8, 128) + surf[t]
        out_ref[1, :, :, at] = register.reshape(5, 16, 128)
        out_ref[0, :, :, at] = mid_ref[:, :, at] + section_b2 * register.reshape(5, 16, 128)
    stores = [
        pltpu.make_async_copy(out_ref.at[0], next_hbm, out_sem.at[0]),
        pltpu.make_async_copy(out_ref.at[1], reg_hbm, out_sem.at[1]),
    ]
    for store in stores:
        store.start()
    for copy in first + second:
        copy.wait_send()
    for store in stores:
        store.wait()


def on_device(
    adjoint, density, velocity, pressure, metric, face_source, face_flip, face_tag, send_list
):
    fields = jnp.transpose(adjoint, (1, 0, 2))
    state = pltpu.VMEM((5, 16, 512), jnp.float32)
    following, register = pl.pallas_call(
        kernel,
        out_shape=[jax.ShapeDtypeStruct((5, 16, 512), jnp.float32)] * 2,
        in_specs=[pl.BlockSpec(memory_space=pl.ANY)] * 11,
        out_specs=[pl.BlockSpec(memory_space=pl.ANY)] * 2,
        scratch_shapes=[
            state, state, state, state,
            pltpu.VMEM((2, 5, 16, 512), jnp.float32),
            pltpu.VMEM((1, 16), jnp.float32),
            pltpu.VMEM((3, 16), jnp.float32),
            pltpu.VMEM((1, 16), jnp.float32),
            pltpu.VMEM((3, 16), jnp.float32),
            pltpu.VMEM((4, 4), jnp.int32),
            pltpu.VMEM((4, 4), jnp.int32),
            pltpu.VMEM((4, 4), jnp.int32),
            pltpu.VMEM((2, 4), jnp.int32),
            pltpu.VMEM((384, 256), jnp.bfloat16),
            pltpu.VMEM((32, 128), jnp.float32),
            pltpu.VMEM((2, 4, 3, 8, 128), jnp.float32),
            pltpu.VMEM((2, 2, 3, 8, 128), jnp.float32),
            pltpu.VMEM((2, 4, 3, 8, 128), jnp.float32),
            pltpu.VMEM((2, 2, 3, 8, 128), jnp.float32),
            pltpu.SemaphoreType.DMA((11,)),
            pltpu.SemaphoreType.DMA((2,)),
            pltpu.SemaphoreType.DMA((2, 6)),
            pltpu.SemaphoreType.DMA((2, 6)),
        ],
        compiler_params=pltpu.CompilerParams(collective_id=0, has_side_effects=True),
        name="sections",
    )(
        fields,
        density.reshape(1, -1),
        velocity,
        pressure.reshape(1, -1),
        metric,
        face_source,
        face_flip,
        face_tag,
        jnp.transpose(send_list),
        jnp.asarray(plane_table()),
        jnp.asarray(depth_table()),
    )
    return jnp.transpose(following, (1, 0, 2)), jnp.transpose(register, (1, 0, 2))


def solution(mesh):
    placed = (
        P(("span", "elem"), None, None),
        P(("span", "elem")),
        P(None, ("span", "elem")),
        P(("span", "elem")),
        P(None, ("span", "elem")),
        P("elem", None),
        P("elem", None),
        P("elem", None),
        P("elem", None),
    )
    return jax.shard_map(
        on_device,
        mesh=mesh,
        in_specs=placed,
        out_specs=(P(("span", "elem"), None, None), P(("span", "elem"), None, None)),
        check_vma=False,
    )
```

```python
import functools

import jax
import jax.numpy as jnp
import numpy as np
from jax import lax
from jax.experimental import pallas as pl
from jax.experimental.pallas import tpu as pltpu
from jax.sharding import PartitionSpec as P

gamma_gas = 1.4
lift_end = 28.0
time_step = 0.02
section_a2 = -567301805773.0 / 1357537059087.0
section_b1 = 1432997174477.0 / 9575080441755.0
section_b2 = 5161836677717.0 / 13612068292357.0
offsets = (1, 2, -1, -2)
MESH = pl.DeviceIdType.MESH


def lobatto_derivative():
    positions = np.array(
        [
            -1.0,
            -0.8717401485096066,
            -0.5917001814331423,
            -0.2092992179024789,
            0.2092992179024789,
            0.5917001814331423,
            0.8717401485096066,
            1.0,
        ]
    )
    total_nodes = positions.shape[0]
    differences = positions[:, None] - positions[None, :] + np.eye(total_nodes)
    weights = 1.0 / np.prod(differences, axis=1)
    matrix_out = weights[None, :] / weights[:, None] / differences
    matrix_out = matrix_out * (1.0 - np.eye(total_nodes))
    return matrix_out - np.eye(total_nodes) * np.sum(matrix_out, axis=1)[:, None]


def plane_table():
    matrix_in = lobatto_derivative()
    along_x = np.kron(np.eye(16), matrix_in).T
    along_y = np.kron(np.eye(2), np.kron(matrix_in, np.eye(8))).T
    table = np.concatenate([along_x, along_y], axis=1).astype(np.float32)
    high = table.astype(jnp.bfloat16)
    low = (table - high.astype(np.float32)).astype(jnp.bfloat16)
    return np.concatenate([high, high, low], axis=0)


def depth_table():
    matrix_in = lobatto_derivative()
    table = np.zeros((4, 4, 2, 128))
    for out_tile in range(4):
        for in_tile in range(4):
            table[out_tile, in_tile, 0, :64] = matrix_in[2 * out_tile, 2 * in_tile]
            table[out_tile, in_tile, 0, 64:] = matrix_in[2 * out_tile + 1, 2 * in_tile + 1]
            table[out_tile, in_tile, 1, :64] = matrix_in[2 * out_tile, 2 * in_tile + 1]
            table[out_tile, in_tile, 1, 64:] = matrix_in[2 * out_tile + 1, 2 * in_tile]
    return table.reshape(32, 128).astype(np.float32)


def along_axis(values, index, axis):
    rest = tuple(a for a in range(values.ndim) if a != axis)
    numbers = lax.GatherDimensionNumbers(
        offset_dims=(),
        collapsed_slice_dims=(axis,),
        start_index_map=(axis,),
        operand_batching_dims=rest,
        start_indices_batching_dims=rest,
    )
    index = jnp.broadcast_to(index, values.shape)
    return lax.gather(
        values,
        index[..., None],
        numbers,
        slice_sizes=(1,) * values.ndim,
        mode=lax.GatherScatterMode.PROMISE_IN_BOUNDS,
    )


def lanes(values, index):
    return along_axis(values, index, values.ndim - 1)


def rows(values, index):
    return along_axis(values, index, values.ndim - 2)


def kernel(
    adj_hbm, rho_hbm, vel_hbm, pres_hbm, met_hbm, src_hbm, flip_hbm, tag_hbm, send_hbm, plane_hbm, depth_hbm,
    next_ref, reg_ref,
    q_ref, mid_ref, keep_ref, acc_ref,
    rho_ref, vel_ref, pres_ref, met_ref, src_ref, flip_ref, tag_ref, send_ref, plane_ref, depth_ref,
    tx_ref, tz_ref, rx_ref, rz_ref,
    in_sem, tx_sem, rx_sem,
):
    n_elem, n_span = lax.axis_size("elem"), lax.axis_size("span")
    part, slab = lax.axis_index("elem"), lax.axis_index("span")
    peers = [{"elem": lax.rem(part + n_elem + o, n_elem)} for o in offsets]
    peers += [{"span": lax.rem(slab + n_span + o, n_span)} for o in (1, -1)]

    barrier = pltpu.get_barrier_semaphore()
    for peer in peers:
        pl.semaphore_signal(barrier, inc=1, device_id=peer, device_id_type=MESH)

    loads = [
        pltpu.make_async_copy(src, dst, in_sem.at[i])
        for i, (src, dst) in enumerate(
            [
                (send_hbm, send_ref), (adj_hbm, q_ref), (plane_hbm, plane_ref), (depth_hbm, depth_ref),
                (rho_hbm, rho_ref), (vel_hbm, vel_ref), (pres_hbm, pres_ref), (met_hbm, met_ref),
                (src_hbm, src_ref), (flip_hbm, flip_ref), (tag_hbm, tag_ref),
            ]
        )
    ]
    for load in loads:
        load.start()

    lane = lax.broadcasted_iota(jnp.int32, (8, 128), 1)
    row = lax.broadcasted_iota(jnp.int32, (8, 128), 0)
    half, place = lane >> 6, lane & 63
    first_half = half == 0
    low_rows = row < 4
    column, group = row & 3, row & 4
    from_x = ((lane >> 3) & 1) * 64 + (lane & 7) * 8 + 7 * half
    from_y = ((lane >> 3) & 1) * 64 + 56 * half + (lane & 7)
    quarter = place >> 4
    node_i, node_j, node_k = lane & 7, (lane >> 3) & 7, lane >> 6
    to_x = 64 * (node_i >> 2) + 8 * node_k + node_j
    to_y = 64 * (node_j >> 2) + 8 * node_k + node_i
    on_x = (node_i == 0) | (node_i == 7)
    on_y = (node_j == 0) | (node_j == 7)

    def tiles_of(ref):
        return [ref[:, :, 128 * t : 128 * t + 128].reshape(10, 8, 128) for t in range(4)]

    def traces(q):
        pair_x, pair_y = lanes(q[0], from_x), lanes(q[0], from_y)
        for t in range(1, 4):
            pair_x = jnp.where(quarter == t, lanes(q[t], from_x), pair_x)
            pair_y = jnp.where(quarter == t, lanes(q[t], from_y), pair_y)
        return pair_x, pair_y, jnp.where(first_half, q[0], q[3])

    def picked(pair_x, pair_y, face):
        index = group + ((face >> 2) & 3)
        return jnp.where((face & 2) == 0, rows(pair_x, index), rows(pair_y, index))

    def send(pair_x, pair_y, swapped, turned, send_faces, turn):
        outs = [
            lanes(picked(pair_x, pair_y, face), 64 * (face & 1) + place) for face in send_faces
        ]
        out = jnp.where(first_half, outs[0], outs[1])
        for j in range(3):
            q = [out[min(4 * j + i, 9)] for i in range(4)]
            odd = (row & 1) == 1
            q = [
                jnp.where(odd, pltpu.roll(q[1], 1, 0), q[0]),
                jnp.where(odd, q[1], pltpu.roll(q[0], 7, 0)),
                jnp.where(odd, pltpu.roll(q[3], 1, 0), q[2]),
                jnp.where(odd, q[3], pltpu.roll(q[2], 7, 0)),
            ]
            upper = (row & 2) == 2
            q = [
                jnp.where(upper, pltpu.roll(q[2], 2, 0), q[0]),
                jnp.where(upper, pltpu.roll(q[3], 2, 0), q[1]),
                jnp.where(upper, q[2], pltpu.roll(q[0], 6, 0)),
                jnp.where(upper, q[3], pltpu.roll(q[1], 6, 0)),
            ]
            for r in range(4):
                tx_ref[turn, r, j] = q[r]
            v0, v1 = 2 * j, min(2 * j + 1, 4)
            tz_ref[turn, 0, j] = jnp.where(low_rows, turned[2 * v0 + 1], swapped[2 * v1 + 1])
            tz_ref[turn, 1, j] = jnp.where(low_rows, swapped[2 * v0], turned[2 * v1])

    def copies(turn):
        return [
            pltpu.make_async_remote_copy(
                src_ref=tx_ref.at[turn, i] if i < 4 else tz_ref.at[turn, i - 4],
                dst_ref=rx_ref.at[turn, i] if i < 4 else rz_ref.at[turn, i - 4],
                send_sem=tx_sem.at[turn, i],
                recv_sem=rx_sem.at[turn, i],
                device_id=peers[i],
                device_id_type=MESH,
            )
            for i in range(6)
        ]

    def volume(q, acc):
        sides = []
        for t in range(4):
            flat = q[t].reshape(80, 128)
            high = flat.astype(jnp.bfloat16)
            low = (flat - high.astype(jnp.float32)).astype(jnp.bfloat16)
            sides.append(jnp.concatenate([high, low, high], axis=1))
        plane = jnp.dot(
            jnp.concatenate(sides, axis=0), plane_ref[...], preferred_element_type=jnp.float32
        )
        rolled = [pltpu.roll(tile, 64, 2) for tile in q]
        for t in range(4):
            depth = None
            for s in range(4):
                for part_in, tile in ((0, q[s]), (1, rolled[s])):
                    at = (t * 4 + s) * 2 + part_in
                    term = depth_ref[at : at + 1, :] * tile
                    depth = term if depth is None else depth + term
            flat = plane[80 * t : 80 * t + 80]
            slopes = [
                flat[:, :128].reshape(5, 2, 8, 128),
                flat[:, 128:].reshape(5, 2, 8, 128),
                depth.reshape(5, 2, 8, 128),
            ]
            total = [
                along[0] * slopes[0][v] + along[1] * slopes[1][v] + along[2] * slopes[2][v]
                for v in range(5)
            ]
            for d in range(3):
                total[1 + d] = total[1 + d] + by_rho[d] * slopes[d][0] + by_stiff[d] * slopes[d][4]
                total[4] = total[4] + by_inverse[d] * slopes[d][1 + d]
            for v in range(5):
                acc[v, :, 128 * t : 128 * t + 128] = total[v].reshape(16, 128)

    def surface(d, difference):
        g = difference.reshape(5, 2, 8, 128)
        out = [face_all[d] * g[v] for v in range(5)]
        out[1 + d] = out[1 + d] + face_rho[d] * g[0] + face_stiff[d] * g[4]
        out[4] = out[4] + face_inverse[d] * g[1 + d]
        return jnp.stack(out, axis=0).reshape(10, 8, 128)

    def lifted(locals_in, pair_x, pair_y, pair_z, turned, turn):
        remote = []
        for r in range(4):
            boxes = [rx_ref[turn, r, j] for j in range(3)]
            remote.append(
                jnp.stack([rows(boxes[vh >> 2], group + (vh & 3)) for vh in range(10)], axis=0)
            )
        pieces = []
        for d, own in ((0, pair_x), (1, pair_y)):
            sides = []
            for f in (2 * d, 2 * d + 1):
                face = sources[f]
                chosen = locals_in[f]
                for r in range(4):
                    chosen = jnp.where((face >> 1) == 8 + r, remote[r], chosen)
                sides.append(lanes(chosen, 64 * (face & 1) + (place ^ (7 * flips[f]))))
            outer = jnp.where(first_half, sides[0], sides[1])
            tag = jnp.where(first_half, tags[2 * d], tags[2 * d + 1])
            plain = jnp.where(tag == 1, 0.0, -1.0)
            normal = jnp.where(tag == 1, -2.0, -1.0)
            own5, outer5 = own.reshape(5, 2, 8, 128), outer.reshape(5, 2, 8, 128)
            difference = jnp.stack(
                [
                    jnp.where(
                        tag == 0, outer5[v] - own5[v], (normal if v == 1 + d else plain) * own5[v]
                    )
                    for v in range(5)
                ],
                axis=0,
            )
            pieces.append(surface(d, difference))
        outers = []
        for v in range(5):
            below, above = rz_ref[turn, 0, v >> 1], rz_ref[turn, 1, v >> 1]
            if v & 1:
                below = pltpu.roll(below, 4, 0)
            else:
                above = pltpu.roll(above, 4, 0)
            t0, t1 = turned[2 * v], turned[2 * v + 1]
            inner = jnp.where(low_rows, t0, t1)
            outers.append(jnp.where(first_half, jnp.where(low_rows, below, t0), inner))
            outers.append(jnp.where(first_half, inner, jnp.where(low_rows, t1, above)))
        piece_z = surface(2, jnp.stack(outers, axis=0) - pair_z)
        result = []
        for t in range(4):
            total = jnp.where(on_x, lanes(pieces[0], to_x + 16 * t), 0.0) + jnp.where(
                on_y, lanes(pieces[1], to_y + 16 * t), 0.0
            )
            if t == 0:
                total = total + jnp.where(first_half, piece_z, 0.0)
            if t == 3:
                total = total + jnp.where(first_half, 0.0, piece_z)
            result.append(total)
        return result

    loads[0].wait()
    loads[1].wait()
    send_faces = []
    for k in range(2):
        face = jnp.zeros((8, 128), jnp.int32)
        for r in range(4):
            face = jnp.where(column == r, send_ref[k : k + 1, r : r + 1], face)
        send_faces.append(face)
    q = tiles_of(q_ref)
    pair_x, pair_y, pair_z = traces(q)
    swapped = pltpu.roll(pair_z, 64, 2)
    turned = pltpu.roll(swapped, 4, 1)
    send(pair_x, pair_y, swapped, turned, send_faces, 0)
    pl.semaphore_wait(barrier, 6)
    first = copies(0)
    for copy in first:
        copy.start()

    for load in loads[2:]:
        load.wait()
    sixteen = lax.broadcasted_iota(jnp.int32, (16, 16), 0) == lax.broadcasted_iota(jnp.int32, (16, 16), 1)

    def upright(line):
        spread = jnp.where(sixteen, jnp.broadcast_to(line, (16, 16)), 0.0)
        return jnp.broadcast_to(jnp.sum(spread, axis=1, keepdims=True), (16, 128)).reshape(2, 8, 128)

    rho, pressure = upright(rho_ref[...]), upright(pres_ref[...])
    stiff = gamma_gas * pressure
    inverse = 1.0 / rho
    sound = jnp.sqrt(stiff / rho)
    sign = jnp.where(first_half, -0.5 * lift_end, 0.5 * lift_end)
    along, by_rho, by_stiff, by_inverse = [], [], [], []
    face_all, face_rho, face_stiff, face_inverse = [], [], [], []
    for d in range(3):
        speed = upright(vel_ref[d : d + 1, :])
        scale = time_step * upright(met_ref[d : d + 1, :])
        along.append(scale * speed)
        by_rho.append(scale * rho)
        by_stiff.append(scale * stiff)
        by_inverse.append(scale * inverse)
        face_all.append(sign * along[d] + 0.5 * lift_end * scale * (jnp.abs(speed) + sound))
        face_rho.append(sign * by_rho[d])
        face_stiff.append(sign * by_stiff[d])
        face_inverse.append(sign * by_inverse[d])

    def spread_column(ref, f):
        one = jnp.broadcast_to(ref[:, f : f + 1], (4, 128))
        return jnp.concatenate([one, one], axis=0)

    sources = [spread_column(src_ref, f) for f in range(4)]
    flips = [spread_column(flip_ref, f) for f in range(4)]
    tags = [spread_column(tag_ref, f) for f in range(4)]

    locals_in = [picked(pair_x, pair_y, sources[f]) for f in range(4)]
    volume(q, acc_ref)
    for copy in first:
        copy.wait_recv()
    surf = lifted(locals_in, pair_x, pair_y, pair_z, turned, 0)
    middle = []
    for t in range(4):
        at = slice(128 * t, 128 * t + 128)
        section = acc_ref[:, :, at].reshape(10, 8, 128) + surf[t]
        middle.append(q_ref[:, :, at].reshape(10, 8, 128) + section_b1 * section)
        mid_ref[:, :, at] = middle[t].reshape(5, 16, 128)
        keep_ref[:, :, at] = (section_a2 * section).reshape(5, 16, 128)

    pair_x, pair_y, pair_z = traces(middle)
    swapped = pltpu.roll(pair_z, 64, 2)
    turned = pltpu.roll(swapped, 4, 1)
    send(pair_x, pair_y, swapped, turned, send_faces, 1)
    second = copies(1)
    for copy in second:
        copy.start()
    locals_in = [picked(pair_x, pair_y, sources[f]) for f in range(4)]
    volume(middle, acc_ref)
    for copy in second:
        copy.wait_recv()
    surf = lifted(locals_in, pair_x, pair_y, pair_z, turned, 1)
    for t in range(4):
        at = slice(128 * t, 128 * t + 128)
        register = (keep_ref[:, :, at] + acc_ref[:, :, at]).reshape(10, 8, 128) + surf[t]
        reg_ref[:, :, at] = register.reshape(5, 16, 128)
        next_ref[:, :, at] = mid_ref[:, :, at] + section_b2 * register.reshape(5, 16, 128)
    for copy in first + second:
        copy.wait_send()


def write(next_in, reg_in, next_out, reg_out, sem):
    stores = [
        pltpu.make_async_copy(next_in, next_out, sem.at[0]),
        pltpu.make_async_copy(reg_in, reg_out, sem.at[1]),
    ]
    for store in stores:
        store.start()
    for store in stores:
        store.wait()


def on_device(
    adjoint, density, velocity, pressure, metric, face_source, face_flip, face_tag, send_list
):
    fields = jnp.transpose(adjoint, (1, 0, 2))
    state = pltpu.VMEM((5, 16, 512), jnp.float32)
    results = pl.pallas_call(
        kernel,
        out_shape=[pltpu.VMEM((5, 16, 512), jnp.float32)] * 2,
        in_specs=[pl.BlockSpec(memory_space=pltpu.HBM)] * 11,
        out_specs=[pl.BlockSpec(memory_space=pltpu.VMEM)] * 2,
        scratch_shapes=[
            state, state, state, state,
            pltpu.VMEM((1, 16), jnp.float32),
            pltpu.VMEM((3, 16), jnp.float32),
            pltpu.VMEM((1, 16), jnp.float32),
            pltpu.VMEM((3, 16), jnp.float32),
            pltpu.VMEM((4, 4), jnp.int32),
            pltpu.VMEM((4, 4), jnp.int32),
            pltpu.VMEM((4, 4), jnp.int32),
            pltpu.VMEM((2, 4), jnp.int32),
            pltpu.VMEM((384, 256), jnp.bfloat16),
            pltpu.VMEM((32, 128), jnp.float32),
            pltpu.VMEM((2, 4, 3, 8, 128), jnp.float32),
            pltpu.VMEM((2, 2, 3, 8, 128), jnp.float32),
            pltpu.VMEM((2, 4, 3, 8, 128), jnp.float32),
            pltpu.VMEM((2, 2, 3, 8, 128), jnp.float32),
            pltpu.SemaphoreType.DMA((11,)),
            pltpu.SemaphoreType.DMA((2, 6)),
            pltpu.SemaphoreType.DMA((2, 6)),
        ],
        compiler_params=pltpu.CompilerParams(collective_id=0, has_side_effects=True),
        name="sections",
    )(
        *(
            pltpu.with_memory_space_constraint(array, pltpu.HBM)
            for array in (
                fields,
                density.reshape(1, -1),
                velocity,
                pressure.reshape(1, -1),
                metric,
                face_source,
                face_flip,
                face_tag,
                jnp.transpose(send_list),
                jnp.asarray(plane_table()),
                jnp.asarray(depth_table()),
            )
        )
    )
    following, register = pl.pallas_call(
        write,
        out_shape=[jax.ShapeDtypeStruct((5, 16, 512), jnp.float32)] * 2,
        in_specs=[pl.BlockSpec(memory_space=pltpu.VMEM)] * 2,
        out_specs=[pl.BlockSpec(memory_space=pltpu.HBM)] * 2,
        scratch_shapes=[pltpu.SemaphoreType.DMA((2,))],
        name="write",
    )(*(pltpu.with_memory_space_constraint(array, pltpu.VMEM) for array in results))
    return jnp.transpose(following, (1, 0, 2)), jnp.transpose(register, (1, 0, 2))


def solution(mesh):
    placed = (
        P(("span", "elem"), None, None),
        P(("span", "elem")),
        P(None, ("span", "elem")),
        P(("span", "elem")),
        P(None, ("span", "elem")),
        P("elem", None),
        P("elem", None),
        P("elem", None),
        P("elem", None),
    )
    return jax.shard_map(
        on_device,
        mesh=mesh,
        in_specs=placed,
        out_specs=(P(("span", "elem"), None, None), P(("span", "elem"), None, None)),
        check_vma=False,
    )
```

```python
import functools

import jax
import jax.numpy as jnp
import numpy as np
from jax import lax
from jax.experimental import pallas as pl
from jax.experimental.pallas import tpu as pltpu
from jax.sharding import PartitionSpec as P

gamma_gas = 1.4
lift_end = 28.0
time_step = 0.02
section_a2 = -567301805773.0 / 1357537059087.0
section_b1 = 1432997174477.0 / 9575080441755.0
section_b2 = 5161836677717.0 / 13612068292357.0
offsets = (1, 2, -1, -2)
line = 32
MESH = pl.DeviceIdType.MESH


def lobatto_derivative():
    positions = np.array(
        [
            -1.0,
            -0.8717401485096066,
            -0.5917001814331423,
            -0.2092992179024789,
            0.2092992179024789,
            0.5917001814331423,
            0.8717401485096066,
            1.0,
        ]
    )
    total_nodes = positions.shape[0]
    differences = positions[:, None] - positions[None, :] + np.eye(total_nodes)
    weights = 1.0 / np.prod(differences, axis=1)
    matrix_out = weights[None, :] / weights[:, None] / differences
    matrix_out = matrix_out * (1.0 - np.eye(total_nodes))
    return matrix_out - np.eye(total_nodes) * np.sum(matrix_out, axis=1)[:, None]


def plane_table():
    matrix_in = lobatto_derivative()
    along_x = np.kron(np.eye(16), matrix_in).T
    along_y = np.kron(np.eye(2), np.kron(matrix_in, np.eye(8))).T
    table = np.concatenate([along_x, along_y], axis=1).astype(np.float32)
    high = table.astype(jnp.bfloat16)
    low = (table - high.astype(np.float32)).astype(jnp.bfloat16)
    return np.concatenate([high, high, low], axis=0)


def depth_table():
    matrix_in = lobatto_derivative()
    table = np.zeros((4, 4, 2, 128))
    for out_tile in range(4):
        for in_tile in range(4):
            table[out_tile, in_tile, 0, :64] = matrix_in[2 * out_tile, 2 * in_tile]
            table[out_tile, in_tile, 0, 64:] = matrix_in[2 * out_tile + 1, 2 * in_tile + 1]
            table[out_tile, in_tile, 1, :64] = matrix_in[2 * out_tile, 2 * in_tile + 1]
            table[out_tile, in_tile, 1, 64:] = matrix_in[2 * out_tile + 1, 2 * in_tile]
    return table.reshape(32, 128).astype(np.float32)


def along_axis(values, index, axis):
    rest = tuple(a for a in range(values.ndim) if a != axis)
    numbers = lax.GatherDimensionNumbers(
        offset_dims=(),
        collapsed_slice_dims=(axis,),
        start_index_map=(axis,),
        operand_batching_dims=rest,
        start_indices_batching_dims=rest,
    )
    index = jnp.broadcast_to(index, values.shape)
    return lax.gather(
        values,
        index[..., None],
        numbers,
        slice_sizes=(1,) * values.ndim,
        mode=lax.GatherScatterMode.PROMISE_IN_BOUNDS,
    )


def lanes(values, index):
    return along_axis(values, index, values.ndim - 1)


def rows(values, index):
    return along_axis(values, index, values.ndim - 2)


def kernel(
    adj_hbm, rho_hbm, vel_hbm, pres_hbm, met_hbm, src_hbm, flip_hbm, tag_hbm, send_hbm, plane_hbm, depth_hbm,
    mid_ref, base_ref, side_ref,
    q_ref, keep_ref, acc_ref,
    rho_ref, vel_ref, pres_ref, met_ref, src_ref, flip_ref, tag_ref, send_ref, plane_ref, depth_ref,
    tx_ref, tz_ref, rx_ref, rz_ref,
    in_sem, tx_sem, rx_sem, rz_sem, pass_sem, late_sem,
):
    n_elem, n_span = lax.axis_size("elem"), lax.axis_size("span")
    part, slab = lax.axis_index("elem"), lax.axis_index("span")
    peers = [{"elem": lax.rem(part + n_elem + o, n_elem)} for o in offsets]
    peers += [{"span": lax.rem(slab + n_span + o, n_span)} for o in (1, -1)]
    spot = lax.rem(part, line)
    begin, begin_next = spot == 0, spot == 1
    end, end_before = spot == line - 1, spot == line - 2
    ones = [x.astype(jnp.int32) for x in (begin, begin_next, end_before, end)]

    def shifted(amount):
        return {"elem": lax.rem(part + n_elem + amount, n_elem)}

    barrier = pltpu.get_barrier_semaphore()

    def greet(peer):
        pl.semaphore_signal(barrier, inc=1, device_id=peer, device_id_type=MESH)

    for i in (3, 2, 4, 5):
        greet(peers[i])

    @pl.when(jnp.logical_not(end))
    def _():
        greet(peers[0])

        @pl.when(jnp.logical_not(end_before))
        def _():
            greet(peers[1])

    @pl.when(begin)
    def _():
        for amount in (line - 1, line - 2, line, line + 1):
            greet(shifted(amount))

    loads = [
        pltpu.make_async_copy(src, dst, in_sem.at[i])
        for i, (src, dst) in enumerate(
            [
                (send_hbm, send_ref), (adj_hbm, q_ref), (plane_hbm, plane_ref), (depth_hbm, depth_ref),
                (rho_hbm, rho_ref), (vel_hbm, vel_ref), (pres_hbm, pres_ref), (met_hbm, met_ref),
                (src_hbm, src_ref), (flip_hbm, flip_ref), (tag_hbm, tag_ref),
            ]
        )
    ]
    for load in loads:
        load.start()

    lane = lax.broadcasted_iota(jnp.int32, (8, 128), 1)
    row = lax.broadcasted_iota(jnp.int32, (8, 128), 0)
    half, place = lane >> 6, lane & 63
    first_half = half == 0
    low_rows = row < 4
    column, group = row & 3, row & 4
    from_x = ((lane >> 3) & 1) * 64 + (lane & 7) * 8 + 7 * half
    from_y = ((lane >> 3) & 1) * 64 + 56 * half + (lane & 7)
    quarter = place >> 4

    def tiles_of(ref):
        return [ref[:, :, 128 * t : 128 * t + 128].reshape(10, 8, 128) for t in range(4)]

    def traces(q):
        pair_x, pair_y = lanes(q[0], from_x), lanes(q[0], from_y)
        for t in range(1, 4):
            pair_x = jnp.where(quarter == t, lanes(q[t], from_x), pair_x)
            pair_y = jnp.where(quarter == t, lanes(q[t], from_y), pair_y)
        return pair_x, pair_y, jnp.where(first_half, q[0], q[3])

    def picked(pair_x, pair_y, face):
        index = group + ((face >> 2) & 3)
        return jnp.where((face & 2) == 0, rows(pair_x, index), rows(pair_y, index))

    def send_sides(pair_x, pair_y, turn):
        outs = [
            lanes(picked(pair_x, pair_y, face), 64 * (face & 1) + place) for face in send_faces
        ]
        out = jnp.where(first_half, outs[0], outs[1])
        odd, upper = (row & 1) == 1, (row & 2) == 2
        for j in range(2):
            q = [out[4 * j + i] for i in range(4)]
            q = [
                jnp.where(odd, pltpu.roll(q[1], 1, 0), q[0]),
                jnp.where(odd, q[1], pltpu.roll(q[0], 7, 0)),
                jnp.where(odd, pltpu.roll(q[3], 1, 0), q[2]),
                jnp.where(odd, q[3], pltpu.roll(q[2], 7, 0)),
            ]
            q = [
                jnp.where(upper, pltpu.roll(q[2], 2, 0), q[0]),
                jnp.where(upper, pltpu.roll(q[3], 2, 0), q[1]),
                jnp.where(upper, q[2], pltpu.roll(q[0], 6, 0)),
                jnp.where(upper, q[3], pltpu.roll(q[1], 6, 0)),
            ]
            for r in range(4):
                tx_ref[turn, r, 8 * j : 8 * j + 8] = q[r]
        for r in range(4):
            index = (row & 2) * 2 + r
            tx_ref[turn, r, 16:24] = jnp.where(odd, rows(out[9], index), rows(out[8], index))

    def send_ends(swapped, turned, turn):
        for j in range(3):
            v0, v1 = 2 * j, min(2 * j + 1, 4)
            tz_ref[turn, 0, 8 * j : 8 * j + 8] = jnp.where(
                low_rows, turned[2 * v0 + 1], swapped[2 * v1 + 1]
            )
            tz_ref[turn, 1, 8 * j : 8 * j + 8] = jnp.where(
                low_rows, swapped[2 * v0], turned[2 * v1]
            )

    def copies(turn):
        return [
            pltpu.make_async_remote_copy(
                src_ref=tx_ref.at[turn, i, 0:20] if i < 4 else tz_ref.at[turn, i - 4, 0:20],
                dst_ref=rx_ref.at[turn, i, 0:20] if i < 4 else rz_ref.at[turn, i - 4, 0:20],
                send_sem=tx_sem.at[turn, i],
                recv_sem=rx_sem.at[turn, i] if i < 4 else rz_sem.at[turn, i - 4],
                device_id=peers[i],
                device_id_type=MESH,
            )
            for i in range(6)
        ]

    def redirected(i, box, target):
        return pltpu.make_async_remote_copy(
            src_ref=tx_ref.at[0, i, 0:20],
            dst_ref=rx_ref.at[0, box, 0:20],
            send_sem=tx_sem.at[0, i],
            recv_sem=rx_sem.at[0, box],
            device_id=target,
            device_id_type=MESH,
        )

    def forwarded(k):
        box, r, amount = ((4, 2, line - 1), (6, 3, line - 1), (5, 3, line - 2))[k]
        return pltpu.make_async_remote_copy(
            src_ref=rx_ref.at[0, box, 0:20],
            dst_ref=rx_ref.at[0, r, 0:20],
            send_sem=pass_sem.at[k],
            recv_sem=rx_sem.at[0, r],
            device_id=shifted(amount),
            device_id_type=MESH,
        )

    def volume(q, acc):
        sides = []
        for t in range(4):
            flat = q[t].reshape(80, 128)
            high = flat.astype(jnp.bfloat16)
            low = (flat - high.astype(jnp.float32)).astype(jnp.bfloat16)
            sides.append(jnp.concatenate([high, low, high], axis=1))
        plane = jnp.dot(
            jnp.concatenate(sides, axis=0), plane_ref[...], preferred_element_type=jnp.float32
        )
        rolled = [pltpu.roll(tile, 64, 2) for tile in q]
        for t in range(4):
            depth = None
            for s in range(4):
                for part_in, tile in ((0, q[s]), (1, rolled[s])):
                    at = (t * 4 + s) * 2 + part_in
                    term = depth_ref[at : at + 1, :] * tile
                    depth = term if depth is None else depth + term
            flat = plane[80 * t : 80 * t + 80]
            slopes = [
                flat[:, :128].reshape(5, 2, 8, 128),
                flat[:, 128:].reshape(5, 2, 8, 128),
                depth.reshape(5, 2, 8, 128),
            ]
            total = [
                along[0] * slopes[0][v] + along[1] * slopes[1][v] + along[2] * slopes[2][v]
                for v in range(5)
            ]
            for d in range(3):
                total[1 + d] = total[1 + d] + by_rho[d] * slopes[d][0] + by_stiff[d] * slopes[d][4]
                total[4] = total[4] + by_inverse[d] * slopes[d][1 + d]
            for v in range(5):
                acc[v, :, 128 * t : 128 * t + 128] = total[v].reshape(16, 128)

    def surface(d, difference):
        g = difference.reshape(5, 2, 8, 128)
        out = [face_all[d] * g[v] for v in range(5)]
        out[1 + d] = out[1 + d] + face_rho[d] * g[0] + face_stiff[d] * g[4]
        out[4] = out[4] + face_inverse[d] * g[1 + d]
        return jnp.stack(out, axis=0).reshape(10, 8, 128)

    def side_pieces(locals_in, pair_x, pair_y, turn):
        remote = []
        for r in range(4):
            boxes = [rx_ref[turn, r, 8 * j : 8 * j + 8] for j in range(3)]
            remote.append(
                jnp.stack(
                    [
                        rows(boxes[vh >> 2], group + (vh & 3) if vh < 8 else (group >> 1) + vh - 8)
                        for vh in range(10)
                    ],
                    axis=0,
                )
            )
        pieces = []
        for d, own in ((0, pair_x), (1, pair_y)):
            sides = []
            for f in (2 * d, 2 * d + 1):
                face = sources[f]
                chosen = locals_in[f]
                for r in range(4):
                    chosen = jnp.where((face >> 1) == 8 + r, remote[r], chosen)
                sides.append(lanes(chosen, 64 * (face & 1) + (place ^ (7 * flips[f]))))
            outer = jnp.where(first_half, sides[0], sides[1])
            tag = jnp.where(first_half, tags[2 * d], tags[2 * d + 1])
            plain = jnp.where(tag == 1, 0.0, -1.0)
            normal = jnp.where(tag == 1, -2.0, -1.0)
            own5, outer5 = own.reshape(5, 2, 8, 128), outer.reshape(5, 2, 8, 128)
            difference = jnp.stack(
                [
                    jnp.where(
                        tag == 0, outer5[v] - own5[v], (normal if v == 1 + d else plain) * own5[v]
                    )
                    for v in range(5)
                ],
                axis=0,
            )
            pieces.append(surface(d, difference))
        return pieces

    def end_piece(pair_z, turned, turn):
        outers = []
        for v in range(5):
            at = 8 * (v >> 1)
            below, above = rz_ref[turn, 0, at : at + 8], rz_ref[turn, 1, at : at + 8]
            if v & 1:
                below = pltpu.roll(below, 4, 0)
            else:
                above = pltpu.roll(above, 4, 0)
            t0, t1 = turned[2 * v], turned[2 * v + 1]
            inner = jnp.where(low_rows, t0, t1)
            outers.append(jnp.where(first_half, jnp.where(low_rows, below, t0), inner))
            outers.append(jnp.where(first_half, inner, jnp.where(low_rows, t1, above)))
        return surface(2, jnp.stack(outers, axis=0) - pair_z)

    def add_ends(piece_z, acc):
        tiles = tiles_of(acc)
        tiles[0] = tiles[0] + jnp.where(first_half, piece_z, 0.0)
        tiles[3] = tiles[3] + jnp.where(first_half, 0.0, piece_z)
        return tiles

    loads[0].wait()
    loads[1].wait()
    send_faces = []
    for k in range(2):
        face = jnp.zeros((8, 128), jnp.int32)
        for r in range(4):
            face = jnp.where(column == r, send_ref[k : k + 1, r : r + 1], face)
        send_faces.append(face)
    q = tiles_of(q_ref)
    pair_x, pair_y, pair_z = traces(q)
    send_sides(pair_x, pair_y, 0)
    swapped = pltpu.roll(pair_z, 64, 2)
    turned = pltpu.roll(swapped, 4, 1)
    send_ends(swapped, turned, 0)
    pl.semaphore_wait(barrier, 6 - ones[0] + ones[2] + ones[3])

    @pl.when(end)
    def _():
        pl.semaphore_signal(late_sem, inc=1, device_id=shifted(1 - line), device_id_type=MESH)

    first = copies(0)
    starts = [
        first[0],
        first[1],
        redirected(2, 2 + 2 * ones[0], shifted(-1 - (line - 1) * ones[0])),
        redirected(
            3,
            3 + 2 * ones[0] + 3 * ones[1],
            shifted(-2 - (line - 2) * ones[0] - (line - 1) * ones[1]),
        ),
    ]
    for i in (1, 3, 0, 2):
        starts[i].start()
    first[4].start()
    first[5].start()

    @pl.when(begin)
    def _():
        for box in (4, 5, 6):
            pltpu.make_async_copy(
                rx_ref.at[0, box, 0:20], rx_ref.at[0, box, 0:20], rx_sem.at[0, box]
            ).wait()
        pl.semaphore_wait(late_sem, 1)
        for k in (2, 1, 0):
            forwarded(k).start()

    for load in loads[2:]:
        load.wait()
    sixteen = lax.broadcasted_iota(jnp.int32, (16, 16), 0) == lax.broadcasted_iota(jnp.int32, (16, 16), 1)

    def upright(line):
        spread = jnp.where(sixteen, jnp.broadcast_to(line, (16, 16)), 0.0)
        return jnp.broadcast_to(jnp.sum(spread, axis=1, keepdims=True), (16, 128)).reshape(2, 8, 128)

    rho, pressure = upright(rho_ref[...]), upright(pres_ref[...])
    stiff = gamma_gas * pressure
    inverse = 1.0 / rho
    sound = jnp.sqrt(stiff / rho)
    sign = jnp.where(first_half, -0.5 * lift_end, 0.5 * lift_end)
    along, by_rho, by_stiff, by_inverse = [], [], [], []
    face_all, face_rho, face_stiff, face_inverse = [], [], [], []
    for d in range(3):
        speed = upright(vel_ref[d : d + 1, :])
        scale = time_step * upright(met_ref[d : d + 1, :])
        along.append(scale * speed)
        by_rho.append(scale * rho)
        by_stiff.append(scale * stiff)
        by_inverse.append(scale * inverse)
        face_all.append(sign * along[d] + 0.5 * lift_end * scale * (jnp.abs(speed) + sound))
        face_rho.append(sign * by_rho[d])
        face_stiff.append(sign * by_stiff[d])
        face_inverse.append(sign * by_inverse[d])

    def spread_column(ref, f):
        one = jnp.broadcast_to(ref[:, f : f + 1], (4, 128))
        return jnp.concatenate([one, one], axis=0)

    sources = [spread_column(src_ref, f) for f in range(4)]
    flips = [spread_column(flip_ref, f) for f in range(4)]
    tags = [spread_column(tag_ref, f) for f in range(4)]

    locals_in = [picked(pair_x, pair_y, sources[f]) for f in range(4)]
    volume(q, acc_ref)
    first[4].wait_recv()
    first[5].wait_recv()
    base = add_ends(end_piece(pair_z, turned, 0), acc_ref)
    for t in range(4):
        acc_ref[:, :, 128 * t : 128 * t + 128] = base[t].reshape(5, 16, 128)
    ahead_x, ahead_y, ahead_z = traces([q[t] + section_b1 * base[t] for t in range(4)])
    for i in (0, 2, 1, 3):
        first[i].wait_recv()
    piece_x, piece_y = side_pieces(locals_in, pair_x, pair_y, 0)
    high, low = place >> 3, place & 7
    low_end, high_end = (low == 0) | (low == 7), (high == 0) | (high == 7)
    across = 64 * (low >> 2) + 8 * high + 7 * half
    pair_x = ahead_x + section_b1 * (piece_x + jnp.where(low_end, lanes(piece_y, across), 0.0))
    pair_y = ahead_y + section_b1 * (piece_y + jnp.where(low_end, lanes(piece_x, across), 0.0))
    send_sides(pair_x, pair_y, 1)
    second = copies(1)
    for i in (1, 3, 0, 2):
        second[i].start()
    pair_z = ahead_z + section_b1 * (
        jnp.where(low_end, lanes(piece_x, 64 * (low >> 2) + 56 * half + high), 0.0)
        + jnp.where(high_end, lanes(piece_y, 64 * (high >> 2) + 56 * half + low), 0.0)
    )
    swapped = pltpu.roll(pair_z, 64, 2)
    turned = pltpu.roll(swapped, 4, 1)
    send_ends(swapped, turned, 1)
    second[4].start()
    second[5].start()

    middle = []
    for t in range(4):
        at = slice(128 * t, 128 * t + 128)
        section = acc_ref[:, :, at].reshape(10, 8, 128) + spread(piece_x, piece_y, t)
        middle.append(q_ref[:, :, at].reshape(10, 8, 128) + section_b1 * section)
        mid_ref[:, :, at] = middle[t].reshape(5, 16, 128)
        keep_ref[:, :, at] = (section_a2 * section).reshape(5, 16, 128)
    locals_in = [picked(pair_x, pair_y, sources[f]) for f in range(4)]
    volume(middle, acc_ref)
    second[4].wait_recv()
    second[5].wait_recv()
    base = add_ends(end_piece(pair_z, turned, 1), acc_ref)
    for t in range(4):
        at = slice(128 * t, 128 * t + 128)
        base_ref[:, :, at] = keep_ref[:, :, at] + base[t].reshape(5, 16, 128)
    for i in (0, 2, 1, 3):
        second[i].wait_recv()
    piece_x, piece_y = side_pieces(locals_in, pair_x, pair_y, 1)
    side_ref[0] = piece_x
    side_ref[1] = piece_y
    for copy in first + second:
        copy.wait_send()

    @pl.when(begin)
    def _():
        for k in range(3):
            forwarded(k).wait_send()


def spread(piece_x, piece_y, t):
    lane = lax.broadcasted_iota(jnp.int32, (8, 128), 1)
    node_i, node_j, node_k = lane & 7, (lane >> 3) & 7, lane >> 6
    to_x = 64 * (node_i >> 2) + 8 * node_k + node_j + 16 * t
    to_y = 64 * (node_j >> 2) + 8 * node_k + node_i + 16 * t
    on_x = (node_i == 0) | (node_i == 7)
    on_y = (node_j == 0) | (node_j == 7)
    return jnp.where(on_x, lanes(piece_x, to_x), 0.0) + jnp.where(on_y, lanes(piece_y, to_y), 0.0)


def finish(mid_in, base_in, side_in, next_hbm, reg_hbm, out_ref, sem):
    stores = []
    for v in range(5):
        piece_x, piece_y = side_in[0, 2 * v : 2 * v + 2], side_in[1, 2 * v : 2 * v + 2]
        for t in range(4):
            at = slice(128 * t, 128 * t + 128)
            register = base_in[v, :, at] + spread(piece_x, piece_y, t).reshape(16, 128)
            out_ref[1, v, :, at] = register
            out_ref[0, v, :, at] = mid_in[v, :, at] + section_b2 * register
        for k, target in enumerate((next_hbm, reg_hbm)):
            stores.append(pltpu.make_async_copy(out_ref.at[k, v], target.at[v], sem.at[k, v]))
            stores[-1].start()
    for store in stores:
        store.wait()


def on_device(
    adjoint, density, velocity, pressure, metric, face_source, face_flip, face_tag, send_list
):
    fields = jnp.transpose(adjoint, (1, 0, 2))
    state = pltpu.VMEM((5, 16, 512), jnp.float32)
    results = pl.pallas_call(
        kernel,
        out_shape=[state, state, pltpu.VMEM((2, 10, 8, 128), jnp.float32)],
        in_specs=[pl.BlockSpec(memory_space=pltpu.HBM)] * 11,
        out_specs=[pl.BlockSpec(memory_space=pltpu.VMEM)] * 3,
        scratch_shapes=[
            state, state, state,
            pltpu.VMEM((1, 16), jnp.float32),
            pltpu.VMEM((3, 16), jnp.float32),
            pltpu.VMEM((1, 16), jnp.float32),
            pltpu.VMEM((3, 16), jnp.float32),
            pltpu.VMEM((4, 4), jnp.int32),
            pltpu.VMEM((4, 4), jnp.int32),
            pltpu.VMEM((4, 4), jnp.int32),
            pltpu.VMEM((2, 4), jnp.int32),
            pltpu.VMEM((384, 256), jnp.bfloat16),
            pltpu.VMEM((32, 128), jnp.float32),
            pltpu.VMEM((2, 4, 24, 128), jnp.float32),
            pltpu.VMEM((2, 2, 24, 128), jnp.float32),
            pltpu.VMEM((2, 7, 24, 128), jnp.float32),
            pltpu.VMEM((2, 2, 24, 128), jnp.float32),
            pltpu.SemaphoreType.DMA((11,)),
            pltpu.SemaphoreType.DMA((2, 6)),
            pltpu.SemaphoreType.DMA((2, 7)),
            pltpu.SemaphoreType.DMA((2, 2)),
            pltpu.SemaphoreType.DMA((3,)),
            pltpu.SemaphoreType.REGULAR,
        ],
        compiler_params=pltpu.CompilerParams(collective_id=0, has_side_effects=True),
        name="sections",
    )(
        *(
            pltpu.with_memory_space_constraint(array, pltpu.HBM)
            for array in (
                fields,
                density.reshape(1, -1),
                velocity,
                pressure.reshape(1, -1),
                metric,
                face_source,
                face_flip,
                face_tag,
                jnp.transpose(send_list),
                jnp.asarray(plane_table()),
                jnp.asarray(depth_table()),
            )
        )
    )
    following, register = pl.pallas_call(
        finish,
        out_shape=[jax.ShapeDtypeStruct((5, 16, 512), jnp.float32)] * 2,
        in_specs=[pl.BlockSpec(memory_space=pltpu.VMEM)] * 3,
        out_specs=[pl.BlockSpec(memory_space=pltpu.HBM)] * 2,
        scratch_shapes=[
            pltpu.VMEM((2, 5, 16, 512), jnp.float32),
            pltpu.SemaphoreType.DMA((2, 5)),
        ],
        name="finish",
    )(*(pltpu.with_memory_space_constraint(array, pltpu.VMEM) for array in results))
    return jnp.transpose(following, (1, 0, 2)), jnp.transpose(register, (1, 0, 2))


def solution(mesh):
    placed = (
        P(("span", "elem"), None, None),
        P(("span", "elem")),
        P(None, ("span", "elem")),
        P(("span", "elem")),
        P(None, ("span", "elem")),
        P("elem", None),
        P("elem", None),
        P("elem", None),
        P("elem", None),
    )
    return jax.shard_map(
        on_device,
        mesh=mesh,
        in_specs=placed,
        out_specs=(P(("span", "elem"), None, None), P(("span", "elem"), None, None)),
        check_vma=False,
    )
```

```python
import functools

import jax
import jax.numpy as jnp
import numpy as np
from jax import lax
from jax.experimental import pallas as pl
from jax.experimental.pallas import tpu as pltpu
from jax.sharding import PartitionSpec as P

gamma_gas = 1.4
lift_end = 28.0
time_step = 0.02
section_a2 = -567301805773.0 / 1357537059087.0
section_b1 = 1432997174477.0 / 9575080441755.0
section_b2 = 5161836677717.0 / 13612068292357.0
offsets = (1, 2, -1, -2)
line = 32
MESH = pl.DeviceIdType.MESH


def lobatto_derivative():
    positions = np.array(
        [
            -1.0,
            -0.8717401485096066,
            -0.5917001814331423,
            -0.2092992179024789,
            0.2092992179024789,
            0.5917001814331423,
            0.8717401485096066,
            1.0,
        ]
    )
    total_nodes = positions.shape[0]
    differences = positions[:, None] - positions[None, :] + np.eye(total_nodes)
    weights = 1.0 / np.prod(differences, axis=1)
    matrix_out = weights[None, :] / weights[:, None] / differences
    matrix_out = matrix_out * (1.0 - np.eye(total_nodes))
    return matrix_out - np.eye(total_nodes) * np.sum(matrix_out, axis=1)[:, None]


def plane_table():
    matrix_in = lobatto_derivative()
    along_x = np.kron(np.eye(16), matrix_in).T
    along_y = np.kron(np.eye(2), np.kron(matrix_in, np.eye(8))).T
    table = np.concatenate([along_x, along_y], axis=1).astype(np.float32)
    high = table.astype(jnp.bfloat16)
    low = (table - high.astype(np.float32)).astype(jnp.bfloat16)
    return np.concatenate([high, high, low], axis=0)


def depth_table():
    matrix_in = lobatto_derivative()
    table = np.zeros((4, 4, 2, 128))
    for out_tile in range(4):
        for in_tile in range(4):
            table[out_tile, in_tile, 0, :64] = matrix_in[2 * out_tile, 2 * in_tile]
            table[out_tile, in_tile, 0, 64:] = matrix_in[2 * out_tile + 1, 2 * in_tile + 1]
            table[out_tile, in_tile, 1, :64] = matrix_in[2 * out_tile, 2 * in_tile + 1]
            table[out_tile, in_tile, 1, 64:] = matrix_in[2 * out_tile + 1, 2 * in_tile]
    return table.reshape(32, 128).astype(np.float32)


def along_axis(values, index, axis):
    rest = tuple(a for a in range(values.ndim) if a != axis)
    numbers = lax.GatherDimensionNumbers(
        offset_dims=(),
        collapsed_slice_dims=(axis,),
        start_index_map=(axis,),
        operand_batching_dims=rest,
        start_indices_batching_dims=rest,
    )
    index = jnp.broadcast_to(index, values.shape)
    return lax.gather(
        values,
        index[..., None],
        numbers,
        slice_sizes=(1,) * values.ndim,
        mode=lax.GatherScatterMode.PROMISE_IN_BOUNDS,
    )


def lanes(values, index):
    return along_axis(values, index, values.ndim - 1)


def rows(values, index):
    return along_axis(values, index, values.ndim - 2)


def kernel(
    adj_hbm, rho_hbm, vel_hbm, pres_hbm, met_hbm, src_hbm, flip_hbm, tag_hbm, send_hbm, plane_hbm, depth_hbm,
    mid_ref, base_ref, side_ref,
    q_ref, keep_ref, acc_ref,
    rho_ref, vel_ref, pres_ref, met_ref, src_ref, flip_ref, tag_ref, send_ref, plane_ref, depth_ref,
    tx_ref, tz_ref, rx_ref, rz_ref,
    in_sem, tx_sem, rx_sem, rz_sem, pass_sem, late_sem, two_sem, span_sem,
):
    n_elem, n_span = lax.axis_size("elem"), lax.axis_size("span")
    part, slab = lax.axis_index("elem"), lax.axis_index("span")
    peers = [{"elem": lax.rem(part + n_elem + o, n_elem)} for o in offsets]
    peers += [{"span": lax.rem(slab + n_span + o, n_span)} for o in (1, -1)]
    spot = lax.rem(part, line)
    begin, begin_next = spot == 0, spot == 1
    end, last_two, last_four = spot == line - 1, spot >= line - 2, spot >= line - 4
    even = lax.rem(slab, 2) == 0
    short = jnp.logical_and(last_two, even)
    one_begin, one_next, one_last, one_short = (
        x.astype(jnp.int32) for x in (begin, begin_next, last_two, short)
    )

    def shifted(amount):
        return {"elem": lax.rem(part + n_elem + amount, n_elem)}

    barrier = pltpu.get_barrier_semaphore()

    def signal(semaphore, peer):
        pl.semaphore_signal(semaphore, inc=1, device_id=peer, device_id_type=MESH)

    signal(barrier, peers[2])

    @pl.when(jnp.logical_not(end))
    def _():
        signal(barrier, peers[0])

    signal(barrier, peers[3])

    @pl.when(jnp.logical_not(last_four))
    def _():
        signal(barrier, peers[1])

    @pl.when(jnp.logical_not(jnp.logical_and(last_two, jnp.logical_not(even))))
    def _():
        signal(barrier, peers[4])
        signal(barrier, peers[5])

    @pl.when(begin)
    def _():
        for amount in (line - 1, line - 2, line, line + 1):
            signal(barrier, shifted(amount))

    loads = [
        pltpu.make_async_copy(src, dst, in_sem.at[i])
        for i, (src, dst) in enumerate(
            [
                (send_hbm, send_ref), (adj_hbm, q_ref), (plane_hbm, plane_ref), (depth_hbm, depth_ref),
                (rho_hbm, rho_ref), (vel_hbm, vel_ref), (pres_hbm, pres_ref), (met_hbm, met_ref),
                (src_hbm, src_ref), (flip_hbm, flip_ref), (tag_hbm, tag_ref),
            ]
        )
    ]
    for load in loads:
        load.start()

    lane = lax.broadcasted_iota(jnp.int32, (8, 128), 1)
    row = lax.broadcasted_iota(jnp.int32, (8, 128), 0)
    half, place = lane >> 6, lane & 63
    first_half = half == 0
    low_rows = row < 4
    column, group = row & 3, row & 4
    from_x = ((lane >> 3) & 1) * 64 + (lane & 7) * 8 + 7 * half
    from_y = ((lane >> 3) & 1) * 64 + 56 * half + (lane & 7)
    quarter = place >> 4

    def tiles_of(ref):
        return [ref[:, :, 128 * t : 128 * t + 128].reshape(10, 8, 128) for t in range(4)]

    def traces(q):
        pair_x, pair_y = lanes(q[0], from_x), lanes(q[0], from_y)
        for t in range(1, 4):
            pair_x = jnp.where(quarter == t, lanes(q[t], from_x), pair_x)
            pair_y = jnp.where(quarter == t, lanes(q[t], from_y), pair_y)
        return pair_x, pair_y, jnp.where(first_half, q[0], q[3])

    def picked(pair_x, pair_y, face):
        index = group + ((face >> 2) & 3)
        return jnp.where((face & 2) == 0, rows(pair_x, index), rows(pair_y, index))

    def send_sides(pair_x, pair_y, turn):
        here, there = [picked(pair_x, pair_y, face) for face in send_faces]
        wanted = jnp.where(first_half, send_faces[0], send_faces[1]) & 1
        out = jnp.where(
            wanted == half,
            jnp.where(first_half, here, there),
            pltpu.roll(jnp.where(first_half, there, here), 64, 2),
        )
        odd, upper = (row & 1) == 1, (row & 2) == 2
        for j in range(2):
            q = [out[4 * j + i] for i in range(4)]
            q = [
                jnp.where(odd, pltpu.roll(q[1], 1, 0), q[0]),
                jnp.where(odd, q[1], pltpu.roll(q[0], 7, 0)),
                jnp.where(odd, pltpu.roll(q[3], 1, 0), q[2]),
                jnp.where(odd, q[3], pltpu.roll(q[2], 7, 0)),
            ]
            q = [
                jnp.where(upper, pltpu.roll(q[2], 2, 0), q[0]),
                jnp.where(upper, pltpu.roll(q[3], 2, 0), q[1]),
                jnp.where(upper, q[2], pltpu.roll(q[0], 6, 0)),
                jnp.where(upper, q[3], pltpu.roll(q[1], 6, 0)),
            ]
            for r in range(4):
                tx_ref[turn, r, 8 * j : 8 * j + 8] = q[r]
        for r in range(4):
            index = (row & 2) * 2 + r
            tx_ref[turn, r, 16:24] = jnp.where(odd, rows(out[9], index), rows(out[8], index))

    def send_ends(swapped, turned, turn):
        for j in range(3):
            v0, v1 = 2 * j, min(2 * j + 1, 4)
            tz_ref[turn, 0, 8 * j : 8 * j + 8] = jnp.where(
                low_rows, turned[2 * v0 + 1], swapped[2 * v1 + 1]
            )
            tz_ref[turn, 1, 8 * j : 8 * j + 8] = jnp.where(
                low_rows, swapped[2 * v0], turned[2 * v1]
            )

    def copies(turn):
        return [
            pltpu.make_async_remote_copy(
                src_ref=tx_ref.at[turn, i, 0:20] if i < 4 else tz_ref.at[turn, i - 4, 0:20],
                dst_ref=rx_ref.at[turn, i, 0:20] if i < 4 else rz_ref.at[turn, i - 4, 0:20],
                send_sem=tx_sem.at[turn, i],
                recv_sem=rx_sem.at[turn, i] if i < 4 else rz_sem.at[turn, i - 4],
                device_id=peers[i],
                device_id_type=MESH,
            )
            for i in range(6)
        ]

    def redirected(i, box, target):
        return pltpu.make_async_remote_copy(
            src_ref=tx_ref.at[0, i, 0:20],
            dst_ref=rx_ref.at[0, box, 0:20],
            send_sem=tx_sem.at[0, i],
            recv_sem=rx_sem.at[0, box],
            device_id=target,
            device_id_type=MESH,
        )

    def forwarded(k):
        box, r, amount = ((4, 2, line - 1), (6, 3, line - 1), (5, 3, line - 2))[k]
        return pltpu.make_async_remote_copy(
            src_ref=rx_ref.at[0, box, 0:20],
            dst_ref=rx_ref.at[0, r, 0:20],
            send_sem=pass_sem.at[k],
            recv_sem=rx_sem.at[0, r],
            device_id=shifted(amount),
            device_id_type=MESH,
        )

    def volume(q, acc):
        sides = []
        for t in range(4):
            flat = q[t].reshape(80, 128)
            high = flat.astype(jnp.bfloat16)
            low = (flat - high.astype(jnp.float32)).astype(jnp.bfloat16)
            sides.append(jnp.concatenate([high, low, high], axis=1))
        plane = jnp.dot(
            jnp.concatenate(sides, axis=0), plane_ref[...], preferred_element_type=jnp.float32
        )
        rolled = [pltpu.roll(tile, 64, 2) for tile in q]
        for t in range(4):
            depth = None
            for s in range(4):
                for part_in, tile in ((0, q[s]), (1, rolled[s])):
                    at = (t * 4 + s) * 2 + part_in
                    term = depth_ref[at : at + 1, :] * tile
                    depth = term if depth is None else depth + term
            flat = plane[80 * t : 80 * t + 80]
            slopes = [
                flat[:, :128].reshape(5, 2, 8, 128),
                flat[:, 128:].reshape(5, 2, 8, 128),
                depth.reshape(5, 2, 8, 128),
            ]
            total = [
                along[0] * slopes[0][v] + along[1] * slopes[1][v] + along[2] * slopes[2][v]
                for v in range(5)
            ]
            for d in range(3):
                total[1 + d] = total[1 + d] + by_rho[d] * slopes[d][0] + by_stiff[d] * slopes[d][4]
                total[4] = total[4] + by_inverse[d] * slopes[d][1 + d]
            for v in range(5):
                acc[v, :, 128 * t : 128 * t + 128] = total[v].reshape(16, 128)

    def surface(d, difference):
        g = difference.reshape(5, 2, 8, 128)
        out = [face_all[d] * g[v] for v in range(5)]
        out[1 + d] = out[1 + d] + face_rho[d] * g[0] + face_stiff[d] * g[4]
        out[4] = out[4] + face_inverse[d] * g[1 + d]
        return jnp.stack(out, axis=0).reshape(10, 8, 128)

    def side_pieces(locals_in, pair_x, pair_y, turn, arrivals, order):
        chosen = list(locals_in)

        def take(r):
            boxes = [rx_ref[turn, r, 8 * j : 8 * j + 8] for j in range(3)]
            remote = jnp.stack(
                [
                    rows(boxes[vh >> 2], group + (vh & 3) if vh < 8 else (group >> 1) + vh - 8)
                    for vh in range(10)
                ],
                axis=0,
            )
            for f in range(4):
                chosen[f] = jnp.where((sources[f] >> 1) == 8 + r, remote, chosen[f])

        for r in order[:3]:
            arrivals[r].wait_recv()
        for r in order[:3]:
            take(r)
        arrivals[order[3]].wait_recv()
        take(order[3])
        pieces = []
        for d, own in ((0, pair_x), (1, pair_y)):
            sides = []
            for f in (2 * d, 2 * d + 1):
                sides.append(lanes(chosen[f], 64 * (sources[f] & 1) + (place ^ (7 * flips[f]))))
            outer = jnp.where(first_half, sides[0], sides[1])
            tag = jnp.where(first_half, tags[2 * d], tags[2 * d + 1])
            plain = jnp.where(tag == 1, 0.0, -1.0)
            normal = jnp.where(tag == 1, -2.0, -1.0)
            own5, outer5 = own.reshape(5, 2, 8, 128), outer.reshape(5, 2, 8, 128)
            difference = jnp.stack(
                [
                    jnp.where(
                        tag == 0, outer5[v] - own5[v], (normal if v == 1 + d else plain) * own5[v]
                    )
                    for v in range(5)
                ],
                axis=0,
            )
            pieces.append(surface(d, difference))
        return pieces

    def end_piece(pair_z, turned, turn):
        outers = []
        for v in range(5):
            at = 8 * (v >> 1)
            below, above = rz_ref[turn, 0, at : at + 8], rz_ref[turn, 1, at : at + 8]
            if v & 1:
                below = pltpu.roll(below, 4, 0)
            else:
                above = pltpu.roll(above, 4, 0)
            t0, t1 = turned[2 * v], turned[2 * v + 1]
            inner = jnp.where(low_rows, t0, t1)
            outers.append(jnp.where(first_half, jnp.where(low_rows, below, t0), inner))
            outers.append(jnp.where(first_half, inner, jnp.where(low_rows, t1, above)))
        return surface(2, jnp.stack(outers, axis=0) - pair_z)

    def add_ends(piece_z, acc):
        tiles = tiles_of(acc)
        tiles[0] = tiles[0] + jnp.where(first_half, piece_z, 0.0)
        tiles[3] = tiles[3] + jnp.where(first_half, 0.0, piece_z)
        return tiles

    loads[0].wait()
    loads[1].wait()
    send_faces = []
    for k in range(2):
        face = jnp.zeros((8, 128), jnp.int32)
        for r in range(4):
            face = jnp.where(column == r, send_ref[k : k + 1, r : r + 1], face)
        send_faces.append(face)
    q = tiles_of(q_ref)
    pair_x, pair_y, pair_z = traces(q)
    send_sides(pair_x, pair_y, 0)
    swapped = pltpu.roll(pair_z, 64, 2)
    turned = pltpu.roll(swapped, 4, 1)
    send_ends(swapped, turned, 0)
    pl.semaphore_wait(barrier, 6 - one_begin - 2 * one_short)

    @pl.when(end)
    def _():
        signal(late_sem, shifted(1 - line))

    @pl.when(jnp.logical_and(last_four, jnp.logical_not(last_two)))
    def _():
        signal(two_sem, peers[1])

    @pl.when(jnp.logical_and(last_two, jnp.logical_not(even)))
    def _():
        signal(span_sem, peers[4])
        signal(span_sem, peers[5])

    first = copies(0)
    back_one = redirected(2, 2 + 2 * one_begin, shifted(-1 - (line - 1) * one_begin))
    back_two = redirected(
        3,
        3 + 2 * one_begin + 3 * one_next,
        shifted(-2 - (line - 2) * one_begin - (line - 1) * one_next),
    )
    first[1].start()

    @pl.when(jnp.logical_not(last_two))
    def _():
        back_two.start()

    first[0].start()
    back_one.start()

    @pl.when(jnp.logical_not(short))
    def _():
        first[4].start()
        first[5].start()

    @pl.when(begin)
    def _():
        for box in (4, 5, 6):
            pltpu.make_async_copy(
                rx_ref.at[0, box, 0:20], rx_ref.at[0, box, 0:20], rx_sem.at[0, box]
            ).wait()
        pl.semaphore_wait(late_sem, 1)
        for k in (2, 1, 0):
            forwarded(k).start()

    for load in loads[2:]:
        load.wait()
    sixteen = lax.broadcasted_iota(jnp.int32, (16, 16), 0) == lax.broadcasted_iota(jnp.int32, (16, 16), 1)

    def upright(line):
        spread = jnp.where(sixteen, jnp.broadcast_to(line, (16, 16)), 0.0)
        return jnp.broadcast_to(jnp.sum(spread, axis=1, keepdims=True), (16, 128)).reshape(2, 8, 128)

    rho, pressure = upright(rho_ref[...]), upright(pres_ref[...])
    stiff = gamma_gas * pressure
    inverse = 1.0 / rho
    sound = jnp.sqrt(stiff / rho)
    sign = jnp.where(first_half, -0.5 * lift_end, 0.5 * lift_end)
    along, by_rho, by_stiff, by_inverse = [], [], [], []
    face_all, face_rho, face_stiff, face_inverse = [], [], [], []
    for d in range(3):
        speed = upright(vel_ref[d : d + 1, :])
        scale = time_step * upright(met_ref[d : d + 1, :])
        along.append(scale * speed)
        by_rho.append(scale * rho)
        by_stiff.append(scale * stiff)
        by_inverse.append(scale * inverse)
        face_all.append(sign * along[d] + 0.5 * lift_end * scale * (jnp.abs(speed) + sound))
        face_rho.append(sign * by_rho[d])
        face_stiff.append(sign * by_stiff[d])
        face_inverse.append(sign * by_inverse[d])

    def spread_column(ref, f):
        one = jnp.broadcast_to(ref[:, f : f + 1], (4, 128))
        return jnp.concatenate([one, one], axis=0)

    sources = [spread_column(src_ref, f) for f in range(4)]
    flips = [spread_column(flip_ref, f) for f in range(4)]
    tags = [spread_column(tag_ref, f) for f in range(4)]

    locals_in = [picked(pair_x, pair_y, sources[f]) for f in range(4)]
    volume(q, acc_ref)

    @pl.when(short)
    def _():
        pl.semaphore_wait(span_sem, 2)
        first[4].start()
        first[5].start()

    first[4].wait_recv()
    first[5].wait_recv()
    base = add_ends(end_piece(pair_z, turned, 0), acc_ref)
    for t in range(4):
        acc_ref[:, :, 128 * t : 128 * t + 128] = base[t].reshape(5, 16, 128)
    ahead_x, ahead_y, ahead_z = traces([q[t] + section_b1 * base[t] for t in range(4)])
    @pl.when(last_two)
    def _():
        pl.semaphore_wait(two_sem, 1)
        back_two.start()

    piece_x, piece_y = side_pieces(locals_in, pair_x, pair_y, 0, first, (0, 1, 2, 3))
    high, low = place >> 3, place & 7
    low_end, high_end = (low == 0) | (low == 7), (high == 0) | (high == 7)
    across = 64 * (low >> 2) + 8 * high + 7 * half
    pair_x = ahead_x + section_b1 * (piece_x + jnp.where(low_end, lanes(piece_y, across), 0.0))
    pair_y = ahead_y + section_b1 * (piece_y + jnp.where(low_end, lanes(piece_x, across), 0.0))
    send_sides(pair_x, pair_y, 1)
    second = copies(1)
    for i in (1, 3, 0, 2):
        second[i].start()
    pair_z = ahead_z + section_b1 * (
        jnp.where(low_end, lanes(piece_x, 64 * (low >> 2) + 56 * half + high), 0.0)
        + jnp.where(high_end, lanes(piece_y, 64 * (high >> 2) + 56 * half + low), 0.0)
    )
    swapped = pltpu.roll(pair_z, 64, 2)
    turned = pltpu.roll(swapped, 4, 1)
    send_ends(swapped, turned, 1)
    second[4].start()
    second[5].start()

    middle = []
    for t in range(4):
        at = slice(128 * t, 128 * t + 128)
        section = acc_ref[:, :, at].reshape(10, 8, 128) + spread(piece_x, piece_y, t)
        middle.append(q_ref[:, :, at].reshape(10, 8, 128) + section_b1 * section)
        mid_ref[:, :, at] = middle[t].reshape(5, 16, 128)
        keep_ref[:, :, at] = (section_a2 * section).reshape(5, 16, 128)
    locals_in = [picked(pair_x, pair_y, sources[f]) for f in range(4)]
    volume(middle, acc_ref)
    second[4].wait_recv()
    second[5].wait_recv()
    base = add_ends(end_piece(pair_z, turned, 1), acc_ref)
    for t in range(4):
        at = slice(128 * t, 128 * t + 128)
        base_ref[:, :, at] = keep_ref[:, :, at] + base[t].reshape(5, 16, 128)
    piece_x, piece_y = side_pieces(locals_in, pair_x, pair_y, 1, second, (0, 2, 3, 1))
    side_ref[0] = piece_x
    side_ref[1] = piece_y
    for copy in first + second:
        copy.wait_send()

    @pl.when(begin)
    def _():
        for k in range(3):
            forwarded(k).wait_send()


def spread(piece_x, piece_y, t):
    lane = lax.broadcasted_iota(jnp.int32, (8, 128), 1)
    node_i, node_j, node_k = lane & 7, (lane >> 3) & 7, lane >> 6
    to_x = 64 * (node_i >> 2) + 8 * node_k + node_j + 16 * t
    to_y = 64 * (node_j >> 2) + 8 * node_k + node_i + 16 * t
    on_x = (node_i == 0) | (node_i == 7)
    on_y = (node_j == 0) | (node_j == 7)
    return jnp.where(on_x, lanes(piece_x, to_x), 0.0) + jnp.where(on_y, lanes(piece_y, to_y), 0.0)


def finish(mid_in, base_in, side_in, next_hbm, reg_hbm, out_ref, sem):
    stores = []
    for v in range(5):
        piece_x, piece_y = side_in[0, 2 * v : 2 * v + 2], side_in[1, 2 * v : 2 * v + 2]
        for t in range(4):
            at = slice(128 * t, 128 * t + 128)
            register = base_in[v, :, at] + spread(piece_x, piece_y, t).reshape(16, 128)
            out_ref[1, v, :, at] = register
            out_ref[0, v, :, at] = mid_in[v, :, at] + section_b2 * register
        for k, target in enumerate((next_hbm, reg_hbm)):
            stores.append(pltpu.make_async_copy(out_ref.at[k, v], target.at[v], sem.at[k, v]))
            stores[-1].start()
    for store in stores:
        store.wait()


def on_device(
    adjoint, density, velocity, pressure, metric, face_source, face_flip, face_tag, send_list
):
    fields = jnp.transpose(adjoint, (1, 0, 2))
    state = pltpu.VMEM((5, 16, 512), jnp.float32)
    results = pl.pallas_call(
        kernel,
        out_shape=[state, state, pltpu.VMEM((2, 10, 8, 128), jnp.float32)],
        in_specs=[pl.BlockSpec(memory_space=pltpu.HBM)] * 11,
        out_specs=[pl.BlockSpec(memory_space=pltpu.VMEM)] * 3,
        scratch_shapes=[
            state, state, state,
            pltpu.VMEM((1, 16), jnp.float32),
            pltpu.VMEM((3, 16), jnp.float32),
            pltpu.VMEM((1, 16), jnp.float32),
            pltpu.VMEM((3, 16), jnp.float32),
            pltpu.VMEM((4, 4), jnp.int32),
            pltpu.VMEM((4, 4), jnp.int32),
            pltpu.VMEM((4, 4), jnp.int32),
            pltpu.VMEM((2, 4), jnp.int32),
            pltpu.VMEM((384, 256), jnp.bfloat16),
            pltpu.VMEM((32, 128), jnp.float32),
            pltpu.VMEM((2, 4, 24, 128), jnp.float32),
            pltpu.VMEM((2, 2, 24, 128), jnp.float32),
            pltpu.VMEM((2, 7, 24, 128), jnp.float32),
            pltpu.VMEM((2, 2, 24, 128), jnp.float32),
            pltpu.SemaphoreType.DMA((11,)),
            pltpu.SemaphoreType.DMA((2, 6)),
            pltpu.SemaphoreType.DMA((2, 7)),
            pltpu.SemaphoreType.DMA((2, 2)),
            pltpu.SemaphoreType.DMA((3,)),
            pltpu.SemaphoreType.REGULAR,
            pltpu.SemaphoreType.REGULAR,
            pltpu.SemaphoreType.REGULAR,
        ],
        compiler_params=pltpu.CompilerParams(collective_id=0, has_side_effects=True),
        name="sections",
    )(
        *(
            pltpu.with_memory_space_constraint(array, pltpu.HBM)
            for array in (
                fields,
                density.reshape(1, -1),
                velocity,
                pressure.reshape(1, -1),
                metric,
                face_source,
                face_flip,
                face_tag,
                jnp.transpose(send_list),
                jnp.asarray(plane_table()),
                jnp.asarray(depth_table()),
            )
        )
    )
    following, register = pl.pallas_call(
        finish,
        out_shape=[jax.ShapeDtypeStruct((5, 16, 512), jnp.float32)] * 2,
        in_specs=[pl.BlockSpec(memory_space=pltpu.VMEM)] * 3,
        out_specs=[pl.BlockSpec(memory_space=pltpu.HBM)] * 2,
        scratch_shapes=[
            pltpu.VMEM((2, 5, 16, 512), jnp.float32),
            pltpu.SemaphoreType.DMA((2, 5)),
        ],
        name="finish",
    )(*(pltpu.with_memory_space_constraint(array, pltpu.VMEM) for array in results))
    return jnp.transpose(following, (1, 0, 2)), jnp.transpose(register, (1, 0, 2))


def solution(mesh):
    placed = (
        P(("span", "elem"), None, None),
        P(("span", "elem")),
        P(None, ("span", "elem")),
        P(("span", "elem")),
        P(None, ("span", "elem")),
        P("elem", None),
        P("elem", None),
        P("elem", None),
        P("elem", None),
    )
    return jax.shard_map(
        on_device,
        mesh=mesh,
        in_specs=placed,
        out_specs=(P(("span", "elem"), None, None), P(("span", "elem"), None, None)),
        check_vma=False,
    )
```

```python
import functools

import jax
import jax.numpy as jnp
import numpy as np
from jax import lax
from jax.experimental import pallas as pl
from jax.experimental.pallas import tpu as pltpu
from jax.sharding import PartitionSpec as P

gamma_gas = 1.4
lift_end = 28.0
time_step = 0.02
section_a2 = -567301805773.0 / 1357537059087.0
section_b1 = 1432997174477.0 / 9575080441755.0
section_b2 = 5161836677717.0 / 13612068292357.0
offsets = (1, 2, -1, -2)
line = 32
MESH = pl.DeviceIdType.MESH


def lobatto_derivative():
    positions = np.array(
        [
            -1.0,
            -0.8717401485096066,
            -0.5917001814331423,
            -0.2092992179024789,
            0.2092992179024789,
            0.5917001814331423,
            0.8717401485096066,
            1.0,
        ]
    )
    total_nodes = positions.shape[0]
    differences = positions[:, None] - positions[None, :] + np.eye(total_nodes)
    weights = 1.0 / np.prod(differences, axis=1)
    matrix_out = weights[None, :] / weights[:, None] / differences
    matrix_out = matrix_out * (1.0 - np.eye(total_nodes))
    return matrix_out - np.eye(total_nodes) * np.sum(matrix_out, axis=1)[:, None]


def plane_table():
    matrix_in = lobatto_derivative()
    along_x = np.kron(np.eye(16), matrix_in).T
    along_y = np.kron(np.eye(2), np.kron(matrix_in, np.eye(8))).T
    table = np.concatenate([along_x, along_y], axis=1).astype(np.float32)
    high = table.astype(jnp.bfloat16)
    low = (table - high.astype(np.float32)).astype(jnp.bfloat16)
    return np.concatenate([high, high, low], axis=0)


def depth_table():
    matrix_in = lobatto_derivative()
    table = np.zeros((4, 4, 2, 128))
    for out_tile in range(4):
        for in_tile in range(4):
            table[out_tile, in_tile, 0, :64] = matrix_in[2 * out_tile, 2 * in_tile]
            table[out_tile, in_tile, 0, 64:] = matrix_in[2 * out_tile + 1, 2 * in_tile + 1]
            table[out_tile, in_tile, 1, :64] = matrix_in[2 * out_tile, 2 * in_tile + 1]
            table[out_tile, in_tile, 1, 64:] = matrix_in[2 * out_tile + 1, 2 * in_tile]
    return table.reshape(32, 128).astype(np.float32)


def along_axis(values, index, axis):
    rest = tuple(a for a in range(values.ndim) if a != axis)
    numbers = lax.GatherDimensionNumbers(
        offset_dims=(),
        collapsed_slice_dims=(axis,),
        start_index_map=(axis,),
        operand_batching_dims=rest,
        start_indices_batching_dims=rest,
    )
    index = jnp.broadcast_to(index, values.shape)
    return lax.gather(
        values,
        index[..., None],
        numbers,
        slice_sizes=(1,) * values.ndim,
        mode=lax.GatherScatterMode.PROMISE_IN_BOUNDS,
    )


def lanes(values, index):
    return along_axis(values, index, values.ndim - 1)


def rows(values, index):
    return along_axis(values, index, values.ndim - 2)


def kernel(
    adj_hbm, rho_hbm, vel_hbm, pres_hbm, met_hbm, src_hbm, flip_hbm, tag_hbm, send_hbm, plane_hbm, depth_hbm,
    mid_ref, base_ref, side_ref,
    q_ref, keep_ref, acc_ref,
    rho_ref, vel_ref, pres_ref, met_ref, src_ref, flip_ref, tag_ref, send_ref, plane_ref, depth_ref,
    tx_ref, tz_ref, rx_ref, rz_ref,
    in_sem, tx_sem, rx_sem, rz_sem, pass_sem, late_sem, two_sem, span_sem,
):
    n_elem, n_span = lax.axis_size("elem"), lax.axis_size("span")
    part, slab = lax.axis_index("elem"), lax.axis_index("span")
    peers = [{"elem": lax.rem(part + n_elem + o, n_elem)} for o in offsets]
    peers += [{"span": lax.rem(slab + n_span + o, n_span)} for o in (1, -1)]
    spot = lax.rem(part, line)
    begin, begin_next = spot == 0, spot == 1
    end, last_two, last_four = spot == line - 1, spot >= line - 2, spot >= line - 4
    even = lax.rem(slab, 2) == 0
    short = jnp.logical_and(last_two, even)
    one_begin, one_next, one_last, one_short = (
        x.astype(jnp.int32) for x in (begin, begin_next, last_two, short)
    )

    def shifted(amount):
        return {"elem": lax.rem(part + n_elem + amount, n_elem)}

    barrier = pltpu.get_barrier_semaphore()

    def signal(semaphore, peer):
        pl.semaphore_signal(semaphore, inc=1, device_id=peer, device_id_type=MESH)

    signal(barrier, peers[2])

    @pl.when(jnp.logical_not(end))
    def _():
        signal(barrier, peers[0])

    signal(barrier, peers[3])

    @pl.when(jnp.logical_not(last_four))
    def _():
        signal(barrier, peers[1])

    @pl.when(jnp.logical_not(jnp.logical_and(last_two, jnp.logical_not(even))))
    def _():
        signal(barrier, peers[4])
        signal(barrier, peers[5])

    @pl.when(begin)
    def _():
        for amount in (line - 1, line - 2, line, line + 1):
            signal(barrier, shifted(amount))

    loads = [
        pltpu.make_async_copy(src, dst, in_sem.at[i])
        for i, (src, dst) in enumerate(
            [
                (send_hbm, send_ref), (adj_hbm, q_ref), (plane_hbm, plane_ref), (depth_hbm, depth_ref),
                (rho_hbm, rho_ref), (vel_hbm, vel_ref), (pres_hbm, pres_ref), (met_hbm, met_ref),
                (src_hbm, src_ref), (flip_hbm, flip_ref), (tag_hbm, tag_ref),
            ]
        )
    ]
    for load in loads:
        load.start()

    lane = lax.broadcasted_iota(jnp.int32, (8, 128), 1)
    row = lax.broadcasted_iota(jnp.int32, (8, 128), 0)
    half, place = lane >> 6, lane & 63
    first_half = half == 0
    low_rows = row < 4
    column, group = row & 3, row & 4
    from_x = ((lane >> 3) & 1) * 64 + (lane & 7) * 8 + 7 * half
    from_y = ((lane >> 3) & 1) * 64 + 56 * half + (lane & 7)
    quarter = place >> 4

    def tiles_of(ref):
        return [ref[:, :, 128 * t : 128 * t + 128].reshape(10, 8, 128) for t in range(4)]

    def traces(q):
        pair_x, pair_y = lanes(q[0], from_x), lanes(q[0], from_y)
        for t in range(1, 4):
            pair_x = jnp.where(quarter == t, lanes(q[t], from_x), pair_x)
            pair_y = jnp.where(quarter == t, lanes(q[t], from_y), pair_y)
        return pair_x, pair_y, jnp.where(first_half, q[0], q[3])

    def picked(pair_x, pair_y, face):
        index = group + ((face >> 2) & 3)
        return jnp.where((face & 2) == 0, rows(pair_x, index), rows(pair_y, index))

    def send_sides(pair_x, pair_y, turn):
        here, there = [picked(pair_x, pair_y, face) for face in send_faces]
        wanted = jnp.where(first_half, send_faces[0], send_faces[1]) & 1
        out = jnp.where(
            wanted == half,
            jnp.where(first_half, here, there),
            pltpu.roll(jnp.where(first_half, there, here), 64, 2),
        )
        odd, upper = (row & 1) == 1, (row & 2) == 2
        for j in range(2):
            q = [out[4 * j + i] for i in range(4)]
            q = [
                jnp.where(odd, pltpu.roll(q[1], 1, 0), q[0]),
                jnp.where(odd, q[1], pltpu.roll(q[0], 7, 0)),
                jnp.where(odd, pltpu.roll(q[3], 1, 0), q[2]),
                jnp.where(odd, q[3], pltpu.roll(q[2], 7, 0)),
            ]
            q = [
                jnp.where(upper, pltpu.roll(q[2], 2, 0), q[0]),
                jnp.where(upper, pltpu.roll(q[3], 2, 0), q[1]),
                jnp.where(upper, q[2], pltpu.roll(q[0], 6, 0)),
                jnp.where(upper, q[3], pltpu.roll(q[1], 6, 0)),
            ]
            for r in range(4):
                tx_ref[turn, r, 8 * j : 8 * j + 8] = q[r]
        for r in range(4):
            index = (row & 2) * 2 + r
            tx_ref[turn, r, 16:24] = jnp.where(odd, rows(out[9], index), rows(out[8], index))

    def send_ends(swapped, turned, turn):
        for j in range(3):
            v0, v1 = 2 * j, min(2 * j + 1, 4)
            tz_ref[turn, 0, 8 * j : 8 * j + 8] = jnp.where(
                low_rows, turned[2 * v0 + 1], swapped[2 * v1 + 1]
            )
            tz_ref[turn, 1, 8 * j : 8 * j + 8] = jnp.where(
                low_rows, swapped[2 * v0], turned[2 * v1]
            )

    def copies(turn):
        return [
            pltpu.make_async_remote_copy(
                src_ref=tx_ref.at[turn, i, 0:20] if i < 4 else tz_ref.at[turn, i - 4, 0:20],
                dst_ref=rx_ref.at[turn, i, 0:20] if i < 4 else rz_ref.at[turn, i - 4, 0:20],
                send_sem=tx_sem.at[turn, i],
                recv_sem=rx_sem.at[turn, i] if i < 4 else rz_sem.at[turn, i - 4],
                device_id=peers[i],
                device_id_type=MESH,
            )
            for i in range(6)
        ]

    def redirected(i, box, target):
        return pltpu.make_async_remote_copy(
            src_ref=tx_ref.at[0, i, 0:20],
            dst_ref=rx_ref.at[0, box, 0:20],
            send_sem=tx_sem.at[0, i],
            recv_sem=rx_sem.at[0, box],
            device_id=target,
            device_id_type=MESH,
        )

    def forwarded(k):
        box, r, amount = ((4, 2, line - 1), (6, 3, line - 1), (5, 3, line - 2))[k]
        return pltpu.make_async_remote_copy(
            src_ref=rx_ref.at[0, box, 0:20],
            dst_ref=rx_ref.at[0, r, 0:20],
            send_sem=pass_sem.at[k],
            recv_sem=rx_sem.at[0, r],
            device_id=shifted(amount),
            device_id_type=MESH,
        )

    def volume(q, acc):
        sides = []
        for t in range(4):
            flat = q[t].reshape(80, 128)
            high = flat.astype(jnp.bfloat16)
            low = (flat - high.astype(jnp.float32)).astype(jnp.bfloat16)
            sides.append(jnp.concatenate([high, low, high], axis=1))
        plane = jnp.dot(
            jnp.concatenate(sides, axis=0), plane_ref[...], preferred_element_type=jnp.float32
        )
        rolled = [pltpu.roll(tile, 64, 2) for tile in q]
        for t in range(4):
            depth = None
            for s in range(4):
                for part_in, tile in ((0, q[s]), (1, rolled[s])):
                    at = (t * 4 + s) * 2 + part_in
                    term = depth_ref[at : at + 1, :] * tile
                    depth = term if depth is None else depth + term
            flat = plane[80 * t : 80 * t + 80]
            slopes = [
                flat[:, :128].reshape(5, 2, 8, 128),
                flat[:, 128:].reshape(5, 2, 8, 128),
                depth.reshape(5, 2, 8, 128),
            ]
            total = [
                along[0] * slopes[0][v] + along[1] * slopes[1][v] + along[2] * slopes[2][v]
                for v in range(5)
            ]
            for d in range(3):
                total[1 + d] = total[1 + d] + by_rho[d] * slopes[d][0] + by_stiff[d] * slopes[d][4]
                total[4] = total[4] + by_inverse[d] * slopes[d][1 + d]
            for v in range(5):
                acc[v, :, 128 * t : 128 * t + 128] = total[v].reshape(16, 128)

    def surface(d, difference):
        g = difference.reshape(5, 2, 8, 128)
        out = [face_all[d] * g[v] for v in range(5)]
        out[1 + d] = out[1 + d] + face_rho[d] * g[0] + face_stiff[d] * g[4]
        out[4] = out[4] + face_inverse[d] * g[1 + d]
        return jnp.stack(out, axis=0).reshape(10, 8, 128)

    def side_pieces(locals_in, pair_x, pair_y, turn, arrivals, order):
        chosen = list(locals_in)

        def take(r):
            boxes = [rx_ref[turn, r, 8 * j : 8 * j + 8] for j in range(3)]
            remote = jnp.stack(
                [
                    rows(boxes[vh >> 2], group + (vh & 3) if vh < 8 else (group >> 1) + vh - 8)
                    for vh in range(10)
                ],
                axis=0,
            )
            for f in range(4):
                chosen[f] = jnp.where((sources[f] >> 1) == 8 + r, remote, chosen[f])

        for r in order[:3]:
            arrivals[r].wait_recv()
        for r in order[:3]:
            take(r)
        arrivals[order[3]].wait_recv()
        take(order[3])
        pieces = []
        for d, own in ((0, pair_x), (1, pair_y)):
            sides = []
            for f in (2 * d, 2 * d + 1):
                sides.append(lanes(chosen[f], 64 * (sources[f] & 1) + (place ^ (7 * flips[f]))))
            outer = jnp.where(first_half, sides[0], sides[1])
            tag = jnp.where(first_half, tags[2 * d], tags[2 * d + 1])
            plain = jnp.where(tag == 1, 0.0, -1.0)
            normal = jnp.where(tag == 1, -2.0, -1.0)
            own5, outer5 = own.reshape(5, 2, 8, 128), outer.reshape(5, 2, 8, 128)
            difference = jnp.stack(
                [
                    jnp.where(
                        tag == 0, outer5[v] - own5[v], (normal if v == 1 + d else plain) * own5[v]
                    )
                    for v in range(5)
                ],
                axis=0,
            )
            pieces.append(surface(d, difference))
        return pieces

    def end_piece(pair_z, turned, turn):
        outers = []
        for v in range(5):
            at = 8 * (v >> 1)
            below, above = rz_ref[turn, 0, at : at + 8], rz_ref[turn, 1, at : at + 8]
            if v & 1:
                below = pltpu.roll(below, 4, 0)
            else:
                above = pltpu.roll(above, 4, 0)
            t0, t1 = turned[2 * v], turned[2 * v + 1]
            inner = jnp.where(low_rows, t0, t1)
            outers.append(jnp.where(first_half, jnp.where(low_rows, below, t0), inner))
            outers.append(jnp.where(first_half, inner, jnp.where(low_rows, t1, above)))
        return surface(2, jnp.stack(outers, axis=0) - pair_z)

    def add_ends(piece_z, acc):
        tiles = tiles_of(acc)
        tiles[0] = tiles[0] + jnp.where(first_half, piece_z, 0.0)
        tiles[3] = tiles[3] + jnp.where(first_half, 0.0, piece_z)
        return tiles

    @pl.when(last_two)
    def _():
        pl.semaphore_wait(barrier, 6 - 2 * one_short)

    @pl.when(end)
    def _():
        signal(late_sem, shifted(1 - line))

    @pl.when(jnp.logical_and(last_two, jnp.logical_not(even)))
    def _():
        signal(span_sem, peers[4])
        signal(span_sem, peers[5])

    loads[0].wait()
    loads[1].wait()
    send_faces = []
    for k in range(2):
        face = jnp.zeros((8, 128), jnp.int32)
        for r in range(4):
            face = jnp.where(column == r, send_ref[k : k + 1, r : r + 1], face)
        send_faces.append(face)
    q = tiles_of(q_ref)
    pair_x, pair_y, pair_z = traces(q)
    send_sides(pair_x, pair_y, 0)
    swapped = pltpu.roll(pair_z, 64, 2)
    turned = pltpu.roll(swapped, 4, 1)
    send_ends(swapped, turned, 0)
    @pl.when(jnp.logical_not(last_two))
    def _():
        pl.semaphore_wait(barrier, 6 - one_begin)

    @pl.when(jnp.logical_and(last_four, jnp.logical_not(last_two)))
    def _():
        signal(two_sem, peers[1])

    first = copies(0)
    back_one = redirected(2, 2 + 2 * one_begin, shifted(-1 - (line - 1) * one_begin))
    back_two = redirected(
        3,
        3 + 2 * one_begin + 3 * one_next,
        shifted(-2 - (line - 2) * one_begin - (line - 1) * one_next),
    )
    first[1].start()

    @pl.when(jnp.logical_not(last_two))
    def _():
        back_two.start()

    first[0].start()
    back_one.start()

    @pl.when(jnp.logical_not(short))
    def _():
        first[4].start()
        first[5].start()

    @pl.when(begin)
    def _():
        for box in (4, 5, 6):
            pltpu.make_async_copy(
                rx_ref.at[0, box, 0:20], rx_ref.at[0, box, 0:20], rx_sem.at[0, box]
            ).wait()
        pl.semaphore_wait(late_sem, 1)
        for k in (2, 1, 0):
            forwarded(k).start()

    for load in loads[2:]:
        load.wait()
    sixteen = lax.broadcasted_iota(jnp.int32, (16, 16), 0) == lax.broadcasted_iota(jnp.int32, (16, 16), 1)

    def upright(line):
        spread = jnp.where(sixteen, jnp.broadcast_to(line, (16, 16)), 0.0)
        return jnp.broadcast_to(jnp.sum(spread, axis=1, keepdims=True), (16, 128)).reshape(2, 8, 128)

    rho, pressure = upright(rho_ref[...]), upright(pres_ref[...])
    stiff = gamma_gas * pressure
    inverse = 1.0 / rho
    sound = jnp.sqrt(stiff / rho)
    sign = jnp.where(first_half, -0.5 * lift_end, 0.5 * lift_end)
    along, by_rho, by_stiff, by_inverse = [], [], [], []
    face_all, face_rho, face_stiff, face_inverse = [], [], [], []
    for d in range(3):
        speed = upright(vel_ref[d : d + 1, :])
        scale = time_step * upright(met_ref[d : d + 1, :])
        along.append(scale * speed)
        by_rho.append(scale * rho)
        by_stiff.append(scale * stiff)
        by_inverse.append(scale * inverse)
        face_all.append(sign * along[d] + 0.5 * lift_end * scale * (jnp.abs(speed) + sound))
        face_rho.append(sign * by_rho[d])
        face_stiff.append(sign * by_stiff[d])
        face_inverse.append(sign * by_inverse[d])

    def spread_column(ref, f):
        one = jnp.broadcast_to(ref[:, f : f + 1], (4, 128))
        return jnp.concatenate([one, one], axis=0)

    sources = [spread_column(src_ref, f) for f in range(4)]
    flips = [spread_column(flip_ref, f) for f in range(4)]
    tags = [spread_column(tag_ref, f) for f in range(4)]

    locals_in = [picked(pair_x, pair_y, sources[f]) for f in range(4)]
    volume(q, acc_ref)

    @pl.when(short)
    def _():
        pl.semaphore_wait(span_sem, 2)
        first[4].start()
        first[5].start()

    first[4].wait_recv()
    first[5].wait_recv()
    base = add_ends(end_piece(pair_z, turned, 0), acc_ref)
    for t in range(4):
        acc_ref[:, :, 128 * t : 128 * t + 128] = base[t].reshape(5, 16, 128)
    ahead_x, ahead_y, ahead_z = traces([q[t] + section_b1 * base[t] for t in range(4)])
    @pl.when(last_two)
    def _():
        pl.semaphore_wait(two_sem, 1)
        back_two.start()

    piece_x, piece_y = side_pieces(locals_in, pair_x, pair_y, 0, first, (0, 1, 2, 3))
    high, low = place >> 3, place & 7
    low_end, high_end = (low == 0) | (low == 7), (high == 0) | (high == 7)
    across = 64 * (low >> 2) + 8 * high + 7 * half
    pair_x = ahead_x + section_b1 * (piece_x + jnp.where(low_end, lanes(piece_y, across), 0.0))
    pair_y = ahead_y + section_b1 * (piece_y + jnp.where(low_end, lanes(piece_x, across), 0.0))
    send_sides(pair_x, pair_y, 1)
    second = copies(1)
    for i in (1, 3, 0, 2):
        second[i].start()
    pair_z = ahead_z + section_b1 * (
        jnp.where(low_end, lanes(piece_x, 64 * (low >> 2) + 56 * half + high), 0.0)
        + jnp.where(high_end, lanes(piece_y, 64 * (high >> 2) + 56 * half + low), 0.0)
    )
    swapped = pltpu.roll(pair_z, 64, 2)
    turned = pltpu.roll(swapped, 4, 1)
    send_ends(swapped, turned, 1)
    second[4].start()
    second[5].start()

    middle = []
    for t in range(4):
        at = slice(128 * t, 128 * t + 128)
        section = acc_ref[:, :, at].reshape(10, 8, 128) + spread(piece_x, piece_y, t)
        middle.append(q_ref[:, :, at].reshape(10, 8, 128) + section_b1 * section)
        mid_ref[:, :, at] = middle[t].reshape(5, 16, 128)
        keep_ref[:, :, at] = (section_a2 * section).reshape(5, 16, 128)
    locals_in = [picked(pair_x, pair_y, sources[f]) for f in range(4)]
    volume(middle, acc_ref)
    second[4].wait_recv()
    second[5].wait_recv()
    base = add_ends(end_piece(pair_z, turned, 1), acc_ref)
    for t in range(4):
        at = slice(128 * t, 128 * t + 128)
        base_ref[:, :, at] = keep_ref[:, :, at] + base[t].reshape(5, 16, 128)
    piece_x, piece_y = side_pieces(locals_in, pair_x, pair_y, 1, second, (0, 2, 3, 1))
    side_ref[0] = piece_x
    side_ref[1] = piece_y
    for copy in first + second:
        copy.wait_send()

    @pl.when(begin)
    def _():
        for k in range(3):
            forwarded(k).wait_send()


def spread(piece_x, piece_y, t):
    lane = lax.broadcasted_iota(jnp.int32, (8, 128), 1)
    node_i, node_j, node_k = lane & 7, (lane >> 3) & 7, lane >> 6
    to_x = 64 * (node_i >> 2) + 8 * node_k + node_j + 16 * t
    to_y = 64 * (node_j >> 2) + 8 * node_k + node_i + 16 * t
    on_x = (node_i == 0) | (node_i == 7)
    on_y = (node_j == 0) | (node_j == 7)
    return jnp.where(on_x, lanes(piece_x, to_x), 0.0) + jnp.where(on_y, lanes(piece_y, to_y), 0.0)


def finish(mid_in, base_in, side_in, next_hbm, reg_hbm, out_ref, sem):
    stores = []
    for v in range(5):
        piece_x, piece_y = side_in[0, 2 * v : 2 * v + 2], side_in[1, 2 * v : 2 * v + 2]
        for t in range(4):
            at = slice(128 * t, 128 * t + 128)
            register = base_in[v, :, at] + spread(piece_x, piece_y, t).reshape(16, 128)
            out_ref[1, v, :, at] = register
            out_ref[0, v, :, at] = mid_in[v, :, at] + section_b2 * register
        for k, target in enumerate((next_hbm, reg_hbm)):
            stores.append(pltpu.make_async_copy(out_ref.at[k, v], target.at[v], sem.at[k, v]))
            stores[-1].start()
    for store in stores:
        store.wait()


def on_device(
    adjoint, density, velocity, pressure, metric, face_source, face_flip, face_tag, send_list
):
    fields = jnp.transpose(adjoint, (1, 0, 2))
    state = pltpu.VMEM((5, 16, 512), jnp.float32)
    results = pl.pallas_call(
        kernel,
        out_shape=[state, state, pltpu.VMEM((2, 10, 8, 128), jnp.float32)],
        in_specs=[pl.BlockSpec(memory_space=pltpu.HBM)] * 11,
        out_specs=[pl.BlockSpec(memory_space=pltpu.VMEM)] * 3,
        scratch_shapes=[
            state, state, state,
            pltpu.VMEM((1, 16), jnp.float32),
            pltpu.VMEM((3, 16), jnp.float32),
            pltpu.VMEM((1, 16), jnp.float32),
            pltpu.VMEM((3, 16), jnp.float32),
            pltpu.VMEM((4, 4), jnp.int32),
            pltpu.VMEM((4, 4), jnp.int32),
            pltpu.VMEM((4, 4), jnp.int32),
            pltpu.VMEM((2, 4), jnp.int32),
            pltpu.VMEM((384, 256), jnp.bfloat16),
            pltpu.VMEM((32, 128), jnp.float32),
            pltpu.VMEM((2, 4, 24, 128), jnp.float32),
            pltpu.VMEM((2, 2, 24, 128), jnp.float32),
            pltpu.VMEM((2, 7, 24, 128), jnp.float32),
            pltpu.VMEM((2, 2, 24, 128), jnp.float32),
            pltpu.SemaphoreType.DMA((11,)),
            pltpu.SemaphoreType.DMA((2, 6)),
            pltpu.SemaphoreType.DMA((2, 7)),
            pltpu.SemaphoreType.DMA((2, 2)),
            pltpu.SemaphoreType.DMA((3,)),
            pltpu.SemaphoreType.REGULAR,
            pltpu.SemaphoreType.REGULAR,
            pltpu.SemaphoreType.REGULAR,
        ],
        compiler_params=pltpu.CompilerParams(collective_id=0, has_side_effects=True),
        name="sections",
    )(
        *(
            pltpu.with_memory_space_constraint(array, pltpu.HBM)
            for array in (
                fields,
                density.reshape(1, -1),
                velocity,
                pressure.reshape(1, -1),
                metric,
                face_source,
                face_flip,
                face_tag,
                jnp.transpose(send_list),
                jnp.asarray(plane_table()),
                jnp.asarray(depth_table()),
            )
        )
    )
    following, register = pl.pallas_call(
        finish,
        out_shape=[jax.ShapeDtypeStruct((5, 16, 512), jnp.float32)] * 2,
        in_specs=[pl.BlockSpec(memory_space=pltpu.VMEM)] * 3,
        out_specs=[pl.BlockSpec(memory_space=pltpu.HBM)] * 2,
        scratch_shapes=[
            pltpu.VMEM((2, 5, 16, 512), jnp.float32),
            pltpu.SemaphoreType.DMA((2, 5)),
        ],
        name="finish",
    )(*(pltpu.with_memory_space_constraint(array, pltpu.VMEM) for array in results))
    return jnp.transpose(following, (1, 0, 2)), jnp.transpose(register, (1, 0, 2))


def solution(mesh):
    placed = (
        P(("span", "elem"), None, None),
        P(("span", "elem")),
        P(None, ("span", "elem")),
        P(("span", "elem")),
        P(None, ("span", "elem")),
        P("elem", None),
        P("elem", None),
        P("elem", None),
        P("elem", None),
    )
    return jax.shard_map(
        on_device,
        mesh=mesh,
        in_specs=placed,
        out_specs=(P(("span", "elem"), None, None), P(("span", "elem"), None, None)),
        check_vma=False,
    )
```

```python
import functools

import jax
import jax.numpy as jnp
import numpy as np
from jax import lax
from jax.experimental import pallas as pl
from jax.experimental.pallas import tpu as pltpu
from jax.sharding import PartitionSpec as P

gamma_gas = 1.4
lift_end = 28.0
time_step = 0.02
section_a2 = -567301805773.0 / 1357537059087.0
section_b1 = 1432997174477.0 / 9575080441755.0
section_b2 = 5161836677717.0 / 13612068292357.0
offsets = (1, 2, -1, -2)
line = 32
MESH = pl.DeviceIdType.MESH


def lobatto_derivative():
    positions = np.array(
        [
            -1.0,
            -0.8717401485096066,
            -0.5917001814331423,
            -0.2092992179024789,
            0.2092992179024789,
            0.5917001814331423,
            0.8717401485096066,
            1.0,
        ]
    )
    total_nodes = positions.shape[0]
    differences = positions[:, None] - positions[None, :] + np.eye(total_nodes)
    weights = 1.0 / np.prod(differences, axis=1)
    matrix_out = weights[None, :] / weights[:, None] / differences
    matrix_out = matrix_out * (1.0 - np.eye(total_nodes))
    return matrix_out - np.eye(total_nodes) * np.sum(matrix_out, axis=1)[:, None]


def plane_table():
    matrix_in = lobatto_derivative()
    along_x = np.kron(np.eye(16), matrix_in).T
    along_y = np.kron(np.eye(2), np.kron(matrix_in, np.eye(8))).T
    table = np.concatenate([along_x, along_y], axis=1).astype(np.float32)
    high = table.astype(jnp.bfloat16)
    low = (table - high.astype(np.float32)).astype(jnp.bfloat16)
    return np.concatenate([high, high, low], axis=0)


def depth_table():
    matrix_in = lobatto_derivative()
    table = np.zeros((4, 4, 2, 128))
    for out_tile in range(4):
        for in_tile in range(4):
            table[out_tile, in_tile, 0, :64] = matrix_in[2 * out_tile, 2 * in_tile]
            table[out_tile, in_tile, 0, 64:] = matrix_in[2 * out_tile + 1, 2 * in_tile + 1]
            table[out_tile, in_tile, 1, :64] = matrix_in[2 * out_tile, 2 * in_tile + 1]
            table[out_tile, in_tile, 1, 64:] = matrix_in[2 * out_tile + 1, 2 * in_tile]
    return table.reshape(32, 128).astype(np.float32)


def along_axis(values, index, axis):
    rest = tuple(a for a in range(values.ndim) if a != axis)
    numbers = lax.GatherDimensionNumbers(
        offset_dims=(),
        collapsed_slice_dims=(axis,),
        start_index_map=(axis,),
        operand_batching_dims=rest,
        start_indices_batching_dims=rest,
    )
    index = jnp.broadcast_to(index, values.shape)
    return lax.gather(
        values,
        index[..., None],
        numbers,
        slice_sizes=(1,) * values.ndim,
        mode=lax.GatherScatterMode.PROMISE_IN_BOUNDS,
    )


def lanes(values, index):
    return along_axis(values, index, values.ndim - 1)


def rows(values, index):
    return along_axis(values, index, values.ndim - 2)


def kernel(
    adj_hbm, rho_hbm, vel_hbm, pres_hbm, met_hbm, src_hbm, flip_hbm, tag_hbm, send_hbm, plane_hbm, depth_hbm,
    mid_ref, base_ref, side_ref,
    q_ref, keep_ref, acc_ref,
    rho_ref, vel_ref, pres_ref, met_ref, src_ref, flip_ref, tag_ref, send_ref, plane_ref, depth_ref,
    tx_ref, tz_ref, rx_ref, rz_ref,
    in_sem, tx_sem, rx_sem, rz_sem, pass_sem, late_sem, two_sem, span_sem,
):
    n_elem, n_span = lax.axis_size("elem"), lax.axis_size("span")
    part, slab = lax.axis_index("elem"), lax.axis_index("span")

    def moved(place_now, amount, size):
        after = place_now + amount
        return after - size * (after >= size).astype(jnp.int32) + size * (after < 0).astype(jnp.int32)

    peers = [{"elem": moved(part, o, n_elem)} for o in offsets]
    peers += [{"span": moved(slab, o, n_span)} for o in (1, -1)]
    spot = lax.rem(part, line)
    begin, begin_next = spot == 0, spot == 1
    end, last_two, last_four = spot == line - 1, spot >= line - 2, spot >= line - 4
    even = lax.rem(slab, 2) == 0
    short = jnp.logical_and(last_two, even)
    one_begin, one_next, one_last, one_short = (
        x.astype(jnp.int32) for x in (begin, begin_next, last_two, short)
    )

    def shifted(amount):
        return {"elem": moved(part, amount, n_elem)}

    barrier = pltpu.get_barrier_semaphore()

    def signal(semaphore, peer):
        pl.semaphore_signal(semaphore, inc=1, device_id=peer, device_id_type=MESH)

    signal(barrier, peers[2])

    @pl.when(jnp.logical_not(end))
    def _():
        signal(barrier, peers[0])

    signal(barrier, peers[3])

    @pl.when(jnp.logical_not(last_four))
    def _():
        signal(barrier, peers[1])

    @pl.when(jnp.logical_not(jnp.logical_and(last_two, jnp.logical_not(even))))
    def _():
        signal(barrier, peers[4])
        signal(barrier, peers[5])

    @pl.when(begin)
    def _():
        for amount in (line - 1, line - 2, line, line + 1):
            signal(barrier, shifted(amount))

    loads = [
        pltpu.make_async_copy(src, dst, in_sem.at[i])
        for i, (src, dst) in enumerate(
            [
                (send_hbm, send_ref), (adj_hbm, q_ref), (plane_hbm, plane_ref), (depth_hbm, depth_ref),
                (rho_hbm, rho_ref), (vel_hbm, vel_ref), (pres_hbm, pres_ref), (met_hbm, met_ref),
                (src_hbm, src_ref), (flip_hbm, flip_ref), (tag_hbm, tag_ref),
            ]
        )
    ]
    for load in loads:
        load.start()

    lane = lax.broadcasted_iota(jnp.int32, (8, 128), 1)
    row = lax.broadcasted_iota(jnp.int32, (8, 128), 0)
    half, place = lane >> 6, lane & 63
    first_half = half == 0
    low_rows = row < 4
    column, group = row & 3, row & 4
    from_x = ((lane >> 3) & 1) * 64 + (lane & 7) * 8 + 7 * half
    from_y = ((lane >> 3) & 1) * 64 + 56 * half + (lane & 7)
    quarter = place >> 4

    def tiles_of(ref):
        return [ref[:, :, 128 * t : 128 * t + 128].reshape(10, 8, 128) for t in range(4)]

    def traces(q):
        pair_x, pair_y = lanes(q[0], from_x), lanes(q[0], from_y)
        for t in range(1, 4):
            pair_x = jnp.where(quarter == t, lanes(q[t], from_x), pair_x)
            pair_y = jnp.where(quarter == t, lanes(q[t], from_y), pair_y)
        return pair_x, pair_y, jnp.where(first_half, q[0], q[3])

    def picked(pair_x, pair_y, face):
        index = group + ((face >> 2) & 3)
        return jnp.where((face & 2) == 0, rows(pair_x, index), rows(pair_y, index))

    def send_sides(pair_x, pair_y, turn):
        here, there = [picked(pair_x, pair_y, face) for face in send_faces]
        wanted = jnp.where(first_half, send_faces[0], send_faces[1]) & 1
        out = jnp.where(
            wanted == half,
            jnp.where(first_half, here, there),
            pltpu.roll(jnp.where(first_half, there, here), 64, 2),
        )
        odd, upper = (row & 1) == 1, (row & 2) == 2
        for j in range(2):
            q = [out[4 * j + i] for i in range(4)]
            q = [
                jnp.where(odd, pltpu.roll(q[1], 1, 0), q[0]),
                jnp.where(odd, q[1], pltpu.roll(q[0], 7, 0)),
                jnp.where(odd, pltpu.roll(q[3], 1, 0), q[2]),
                jnp.where(odd, q[3], pltpu.roll(q[2], 7, 0)),
            ]
            q = [
                jnp.where(upper, pltpu.roll(q[2], 2, 0), q[0]),
                jnp.where(upper, pltpu.roll(q[3], 2, 0), q[1]),
                jnp.where(upper, q[2], pltpu.roll(q[0], 6, 0)),
                jnp.where(upper, q[3], pltpu.roll(q[1], 6, 0)),
            ]
            for r in range(4):
                tx_ref[turn, r, 8 * j : 8 * j + 8] = q[r]
        for r in range(4):
            index = (row & 2) * 2 + r
            tx_ref[turn, r, 16:24] = jnp.where(odd, rows(out[9], index), rows(out[8], index))

    def send_ends(swapped, turned, turn):
        for j in range(3):
            v0, v1 = 2 * j, min(2 * j + 1, 4)
            tz_ref[turn, 0, 8 * j : 8 * j + 8] = jnp.where(
                low_rows, turned[2 * v0 + 1], swapped[2 * v1 + 1]
            )
            tz_ref[turn, 1, 8 * j : 8 * j + 8] = jnp.where(
                low_rows, swapped[2 * v0], turned[2 * v1]
            )

    def copies(turn):
        return [
            pltpu.make_async_remote_copy(
                src_ref=tx_ref.at[turn, i, 0:20] if i < 4 else tz_ref.at[turn, i - 4, 0:20],
                dst_ref=rx_ref.at[turn, i, 0:20] if i < 4 else rz_ref.at[turn, i - 4, 0:20],
                send_sem=tx_sem.at[turn, i],
                recv_sem=rx_sem.at[turn, i] if i < 4 else rz_sem.at[turn, i - 4],
                device_id=peers[i],
                device_id_type=MESH,
            )
            for i in range(6)
        ]

    def redirected(i, box, target):
        return pltpu.make_async_remote_copy(
            src_ref=tx_ref.at[0, i, 0:20],
            dst_ref=rx_ref.at[0, box, 0:20],
            send_sem=tx_sem.at[0, i],
            recv_sem=rx_sem.at[0, box],
            device_id=target,
            device_id_type=MESH,
        )

    def forwarded(k):
        box, r, amount = ((4, 2, line - 1), (6, 3, line - 1), (5, 3, line - 2))[k]
        return pltpu.make_async_remote_copy(
            src_ref=rx_ref.at[0, box, 0:20],
            dst_ref=rx_ref.at[0, r, 0:20],
            send_sem=pass_sem.at[k],
            recv_sem=rx_sem.at[0, r],
            device_id=shifted(amount),
            device_id_type=MESH,
        )

    def volume(q, acc):
        sides = []
        for t in range(4):
            flat = q[t].reshape(80, 128)
            high = flat.astype(jnp.bfloat16)
            low = (flat - high.astype(jnp.float32)).astype(jnp.bfloat16)
            sides.append(jnp.concatenate([high, low, high], axis=1))
        plane = jnp.dot(
            jnp.concatenate(sides, axis=0), plane_ref[...], preferred_element_type=jnp.float32
        )
        rolled = [pltpu.roll(tile, 64, 2) for tile in q]
        for t in range(4):
            depth = None
            for s in range(4):
                for part_in, tile in ((0, q[s]), (1, rolled[s])):
                    at = (t * 4 + s) * 2 + part_in
                    term = depth_ref[at : at + 1, :] * tile
                    depth = term if depth is None else depth + term
            flat = plane[80 * t : 80 * t + 80]
            slopes = [
                flat[:, :128].reshape(5, 2, 8, 128),
                flat[:, 128:].reshape(5, 2, 8, 128),
                depth.reshape(5, 2, 8, 128),
            ]
            total = [
                along[0] * slopes[0][v] + along[1] * slopes[1][v] + along[2] * slopes[2][v]
                for v in range(5)
            ]
            for d in range(3):
                total[1 + d] = total[1 + d] + by_rho[d] * slopes[d][0] + by_stiff[d] * slopes[d][4]
                total[4] = total[4] + by_inverse[d] * slopes[d][1 + d]
            for v in range(5):
                acc[v, :, 128 * t : 128 * t + 128] = total[v].reshape(16, 128)

    def surface(d, difference):
        g = difference.reshape(5, 2, 8, 128)
        out = [face_all[d] * g[v] for v in range(5)]
        out[1 + d] = out[1 + d] + face_rho[d] * g[0] + face_stiff[d] * g[4]
        out[4] = out[4] + face_inverse[d] * g[1 + d]
        return jnp.stack(out, axis=0).reshape(10, 8, 128)

    def side_pieces(locals_in, pair_x, pair_y, turn, arrivals, order):
        chosen = list(locals_in)

        def take(r):
            boxes = [rx_ref[turn, r, 8 * j : 8 * j + 8] for j in range(3)]
            remote = jnp.stack(
                [
                    rows(boxes[vh >> 2], group + (vh & 3) if vh < 8 else (group >> 1) + vh - 8)
                    for vh in range(10)
                ],
                axis=0,
            )
            for f in range(4):
                chosen[f] = jnp.where((sources[f] >> 1) == 8 + r, remote, chosen[f])

        for r in order[:3]:
            arrivals[r].wait_recv()
        for r in order[:3]:
            take(r)
        arrivals[order[3]].wait_recv()
        take(order[3])
        pieces = []
        for d, own in ((0, pair_x), (1, pair_y)):
            sides = []
            for f in (2 * d, 2 * d + 1):
                sides.append(lanes(chosen[f], 64 * (sources[f] & 1) + (place ^ (7 * flips[f]))))
            outer = jnp.where(first_half, sides[0], sides[1])
            tag = jnp.where(first_half, tags[2 * d], tags[2 * d + 1])
            plain = jnp.where(tag == 1, 0.0, -1.0)
            normal = jnp.where(tag == 1, -2.0, -1.0)
            own5, outer5 = own.reshape(5, 2, 8, 128), outer.reshape(5, 2, 8, 128)
            difference = jnp.stack(
                [
                    jnp.where(
                        tag == 0, outer5[v] - own5[v], (normal if v == 1 + d else plain) * own5[v]
                    )
                    for v in range(5)
                ],
                axis=0,
            )
            pieces.append(surface(d, difference))
        return pieces

    def end_piece(pair_z, turned, turn):
        outers = []
        for v in range(5):
            at = 8 * (v >> 1)
            below, above = rz_ref[turn, 0, at : at + 8], rz_ref[turn, 1, at : at + 8]
            if v & 1:
                below = pltpu.roll(below, 4, 0)
            else:
                above = pltpu.roll(above, 4, 0)
            t0, t1 = turned[2 * v], turned[2 * v + 1]
            inner = jnp.where(low_rows, t0, t1)
            outers.append(jnp.where(first_half, jnp.where(low_rows, below, t0), inner))
            outers.append(jnp.where(first_half, inner, jnp.where(low_rows, t1, above)))
        return surface(2, jnp.stack(outers, axis=0) - pair_z)

    def add_ends(piece_z, acc):
        tiles = tiles_of(acc)
        tiles[0] = tiles[0] + jnp.where(first_half, piece_z, 0.0)
        tiles[3] = tiles[3] + jnp.where(first_half, 0.0, piece_z)
        return tiles

    @pl.when(last_two)
    def _():
        pl.semaphore_wait(barrier, 6 - 2 * one_short)

    @pl.when(end)
    def _():
        signal(late_sem, shifted(1 - line))

    @pl.when(jnp.logical_and(last_two, jnp.logical_not(even)))
    def _():
        signal(span_sem, peers[4])
        signal(span_sem, peers[5])

    loads[0].wait()
    loads[1].wait()
    send_faces = []
    for k in range(2):
        face = jnp.zeros((8, 128), jnp.int32)
        for r in range(4):
            face = jnp.where(column == r, send_ref[k : k + 1, r : r + 1], face)
        send_faces.append(face)
    q = tiles_of(q_ref)
    pair_x, pair_y, pair_z = traces(q)
    send_sides(pair_x, pair_y, 0)
    swapped = pltpu.roll(pair_z, 64, 2)
    turned = pltpu.roll(swapped, 4, 1)
    send_ends(swapped, turned, 0)
    @pl.when(jnp.logical_not(last_two))
    def _():
        pl.semaphore_wait(barrier, 6 - one_begin)

    @pl.when(jnp.logical_and(last_four, jnp.logical_not(last_two)))
    def _():
        signal(two_sem, peers[1])

    first = copies(0)
    back_one = redirected(2, 2 + 2 * one_begin, shifted(-1 - (line - 1) * one_begin))
    back_two = redirected(
        3,
        3 + 2 * one_begin + 3 * one_next,
        shifted(-2 - (line - 2) * one_begin - (line - 1) * one_next),
    )
    first[1].start()

    @pl.when(jnp.logical_not(last_two))
    def _():
        back_two.start()

    first[0].start()
    back_one.start()

    @pl.when(jnp.logical_not(short))
    def _():
        first[4].start()
        first[5].start()

    @pl.when(begin)
    def _():
        for box in (4, 5, 6):
            pltpu.make_async_copy(
                rx_ref.at[0, box, 0:20], rx_ref.at[0, box, 0:20], rx_sem.at[0, box]
            ).wait()
        pl.semaphore_wait(late_sem, 1)
        for k in (2, 1, 0):
            forwarded(k).start()

    for load in loads[2:]:
        load.wait()
    sixteen = lax.broadcasted_iota(jnp.int32, (16, 16), 0) == lax.broadcasted_iota(jnp.int32, (16, 16), 1)

    def upright(line):
        spread = jnp.where(sixteen, jnp.broadcast_to(line, (16, 16)), 0.0)
        return jnp.broadcast_to(jnp.sum(spread, axis=1, keepdims=True), (16, 128)).reshape(2, 8, 128)

    rho, pressure = upright(rho_ref[...]), upright(pres_ref[...])
    stiff = gamma_gas * pressure
    inverse = 1.0 / rho
    sound = jnp.sqrt(stiff / rho)
    sign = jnp.where(first_half, -0.5 * lift_end, 0.5 * lift_end)
    along, by_rho, by_stiff, by_inverse = [], [], [], []
    face_all, face_rho, face_stiff, face_inverse = [], [], [], []
    for d in range(3):
        speed = upright(vel_ref[d : d + 1, :])
        scale = time_step * upright(met_ref[d : d + 1, :])
        along.append(scale * speed)
        by_rho.append(scale * rho)
        by_stiff.append(scale * stiff)
        by_inverse.append(scale * inverse)
        face_all.append(sign * along[d] + 0.5 * lift_end * scale * (jnp.abs(speed) + sound))
        face_rho.append(sign * by_rho[d])
        face_stiff.append(sign * by_stiff[d])
        face_inverse.append(sign * by_inverse[d])

    def spread_column(ref, f):
        one = jnp.broadcast_to(ref[:, f : f + 1], (4, 128))
        return jnp.concatenate([one, one], axis=0)

    sources = [spread_column(src_ref, f) for f in range(4)]
    flips = [spread_column(flip_ref, f) for f in range(4)]
    tags = [spread_column(tag_ref, f) for f in range(4)]

    locals_in = [picked(pair_x, pair_y, sources[f]) for f in range(4)]
    volume(q, acc_ref)

    @pl.when(short)
    def _():
        pl.semaphore_wait(span_sem, 2)
        first[4].start()
        first[5].start()

    first[4].wait_recv()
    first[5].wait_recv()
    base = add_ends(end_piece(pair_z, turned, 0), acc_ref)
    for t in range(4):
        acc_ref[:, :, 128 * t : 128 * t + 128] = base[t].reshape(5, 16, 128)
    ahead_x, ahead_y, ahead_z = traces([q[t] + section_b1 * base[t] for t in range(4)])
    @pl.when(last_two)
    def _():
        pl.semaphore_wait(two_sem, 1)
        back_two.start()

    piece_x, piece_y = side_pieces(locals_in, pair_x, pair_y, 0, first, (0, 1, 2, 3))
    high, low = place >> 3, place & 7
    low_end, high_end = (low == 0) | (low == 7), (high == 0) | (high == 7)
    across = 64 * (low >> 2) + 8 * high + 7 * half
    pair_x = ahead_x + section_b1 * (piece_x + jnp.where(low_end, lanes(piece_y, across), 0.0))
    pair_y = ahead_y + section_b1 * (piece_y + jnp.where(low_end, lanes(piece_x, across), 0.0))
    send_sides(pair_x, pair_y, 1)
    second = copies(1)
    for i in (1, 3, 0, 2):
        second[i].start()
    pair_z = ahead_z + section_b1 * (
        jnp.where(low_end, lanes(piece_x, 64 * (low >> 2) + 56 * half + high), 0.0)
        + jnp.where(high_end, lanes(piece_y, 64 * (high >> 2) + 56 * half + low), 0.0)
    )
    swapped = pltpu.roll(pair_z, 64, 2)
    turned = pltpu.roll(swapped, 4, 1)
    send_ends(swapped, turned, 1)
    second[4].start()
    second[5].start()

    middle = []
    for t in range(4):
        at = slice(128 * t, 128 * t + 128)
        section = acc_ref[:, :, at].reshape(10, 8, 128) + spread(piece_x, piece_y, t)
        middle.append(q_ref[:, :, at].reshape(10, 8, 128) + section_b1 * section)
        mid_ref[:, :, at] = middle[t].reshape(5, 16, 128)
        keep_ref[:, :, at] = (section_a2 * section).reshape(5, 16, 128)
    locals_in = [picked(pair_x, pair_y, sources[f]) for f in range(4)]
    volume(middle, acc_ref)
    for copy in first:
        copy.wait_send()

    @pl.when(begin)
    def _():
        for k in range(3):
            forwarded(k).wait_send()

    second[4].wait_recv()
    second[5].wait_recv()
    base = add_ends(end_piece(pair_z, turned, 1), acc_ref)
    for t in range(4):
        at = slice(128 * t, 128 * t + 128)
        base_ref[:, :, at] = keep_ref[:, :, at] + base[t].reshape(5, 16, 128)
    piece_x, piece_y = side_pieces(locals_in, pair_x, pair_y, 1, second, (0, 2, 3, 1))
    side_ref[0] = piece_x
    side_ref[1] = piece_y
    for copy in second:
        copy.wait_send()


def spread(piece_x, piece_y, t):
    lane = lax.broadcasted_iota(jnp.int32, (8, 128), 1)
    node_i, node_j, node_k = lane & 7, (lane >> 3) & 7, lane >> 6
    to_x = 64 * (node_i >> 2) + 8 * node_k + node_j + 16 * t
    to_y = 64 * (node_j >> 2) + 8 * node_k + node_i + 16 * t
    on_x = (node_i == 0) | (node_i == 7)
    on_y = (node_j == 0) | (node_j == 7)
    return jnp.where(on_x, lanes(piece_x, to_x), 0.0) + jnp.where(on_y, lanes(piece_y, to_y), 0.0)


def finish(mid_in, base_in, side_in, next_hbm, reg_hbm, out_ref, sem):
    stores = []
    for begin_v, end_v in ((0, 3), (3, 5)):
        some = slice(begin_v, end_v)
        piece_x, piece_y = (side_in[k, 2 * begin_v : 2 * end_v] for k in range(2))
        for t in range(4):
            at = slice(128 * t, 128 * t + 128)
            added = spread(piece_x, piece_y, t).reshape(end_v - begin_v, 16, 128)
            register = base_in[some, :, at] + added
            out_ref[1, some, :, at] = register
            out_ref[0, some, :, at] = mid_in[some, :, at] + section_b2 * register
        for k, target in enumerate((next_hbm, reg_hbm)):
            stores.append(
                pltpu.make_async_copy(out_ref.at[k, some], target.at[some], sem.at[k, begin_v])
            )
            stores[-1].start()
    for store in stores:
        store.wait()


def on_device(
    adjoint, density, velocity, pressure, metric, face_source, face_flip, face_tag, send_list
):
    fields = jnp.transpose(adjoint, (1, 0, 2))
    state = pltpu.VMEM((5, 16, 512), jnp.float32)
    results = pl.pallas_call(
        kernel,
        out_shape=[state, state, pltpu.VMEM((2, 10, 8, 128), jnp.float32)],
        in_specs=[pl.BlockSpec(memory_space=pltpu.HBM)] * 11,
        out_specs=[pl.BlockSpec(memory_space=pltpu.VMEM)] * 3,
        scratch_shapes=[
            state, state, state,
            pltpu.VMEM((1, 16), jnp.float32),
            pltpu.VMEM((3, 16), jnp.float32),
            pltpu.VMEM((1, 16), jnp.float32),
            pltpu.VMEM((3, 16), jnp.float32),
            pltpu.VMEM((4, 4), jnp.int32),
            pltpu.VMEM((4, 4), jnp.int32),
            pltpu.VMEM((4, 4), jnp.int32),
            pltpu.VMEM((2, 4), jnp.int32),
            pltpu.VMEM((384, 256), jnp.bfloat16),
            pltpu.VMEM((32, 128), jnp.float32),
            pltpu.VMEM((2, 4, 24, 128), jnp.float32),
            pltpu.VMEM((2, 2, 24, 128), jnp.float32),
            pltpu.VMEM((2, 7, 24, 128), jnp.float32),
            pltpu.VMEM((2, 2, 24, 128), jnp.float32),
            pltpu.SemaphoreType.DMA((11,)),
            pltpu.SemaphoreType.DMA((2, 6)),
            pltpu.SemaphoreType.DMA((2, 7)),
            pltpu.SemaphoreType.DMA((2, 2)),
            pltpu.SemaphoreType.DMA((3,)),
            pltpu.SemaphoreType.REGULAR,
            pltpu.SemaphoreType.REGULAR,
            pltpu.SemaphoreType.REGULAR,
        ],
        compiler_params=pltpu.CompilerParams(collective_id=0, has_side_effects=True),
        name="sections",
    )(
        *(
            pltpu.with_memory_space_constraint(array, pltpu.HBM)
            for array in (
                fields,
                density.reshape(1, -1),
                velocity,
                pressure.reshape(1, -1),
                metric,
                face_source,
                face_flip,
                face_tag,
                jnp.transpose(send_list),
                jnp.asarray(plane_table()),
                jnp.asarray(depth_table()),
            )
        )
    )
    following, register = pl.pallas_call(
        finish,
        out_shape=[jax.ShapeDtypeStruct((5, 16, 512), jnp.float32)] * 2,
        in_specs=[pl.BlockSpec(memory_space=pltpu.VMEM)] * 3,
        out_specs=[pl.BlockSpec(memory_space=pltpu.HBM)] * 2,
        scratch_shapes=[
            pltpu.VMEM((2, 5, 16, 512), jnp.float32),
            pltpu.SemaphoreType.DMA((2, 5)),
        ],
        name="finish",
    )(*(pltpu.with_memory_space_constraint(array, pltpu.VMEM) for array in results))
    return jnp.transpose(following, (1, 0, 2)), jnp.transpose(register, (1, 0, 2))


def solution(mesh):
    placed = (
        P(("span", "elem"), None, None),
        P(("span", "elem")),
        P(None, ("span", "elem")),
        P(("span", "elem")),
        P(None, ("span", "elem")),
        P("elem", None),
        P("elem", None),
        P("elem", None),
        P("elem", None),
    )
    return jax.shard_map(
        on_device,
        mesh=mesh,
        in_specs=placed,
        out_specs=(P(("span", "elem"), None, None), P(("span", "elem"), None, None)),
        check_vma=False,
    )
```
